512 devices in a mesh: subj: 32 (over y, z_lo), slab: 16 (over x, z_hi, core).
Axes of the slice: x: 4, y: 4, z: 16 (z_hi: 2, z_lo: 8; z = z_hi * 8 + z_lo), core: 2. Of those that a mesh axis runs over, the one named last changes fastest.
Arguments:
- image: float32 [32, 192, 32, 192], P('subj', 'slab'), may hold values from -6 to 6
- velocity: float32 [32, 3, 192, 32, 192], P('subj', None, 'slab'), may hold values from -3 to 3
- template: float32 [192, 32, 192], P('slab', 'subj'), may hold values from -6 to 6
- z_kernel: float32 [192, 192], replicated, as said below
- x_kernel: float32 [192, 192], replicated, as said below
Outputs:
- velocity_update: float32 [32, 3, 192, 32, 192], P('subj', None, 'slab')
- new_template: float32 [192, 32, 192], P('slab', 'subj')
The draws below stay inside these ranges and needn't reach their ends.
Inputs may be any that keep to these rules, and one draw needn't show every extreme that they name: `z_kernel`: entries are positive. `x_kernel`: entries are positive.
All inputs are finite; a program needn't handle non-finite values.
Results may differ from the reference program's by a relative error of at most 0.00028.
Values sent between devices are 32-bit elements; how exact they have to be, the bound alone decides.
No kernel may reach another device: no remote copies, remote signals or barrier semaphores. Data moves between devices by JAX's collectives and lax.ppermute only.
A program may use at most 64 MiB of HBM per device.

```python
import math
import jax
import jax.numpy as jnp
from jax import lax

NZ = 192
NX = 192
SUBJECTS = 32
YW = 32


def kernel_draw(key, length):
    indices = jnp.arange(length, dtype=jnp.float32)
    distance = jnp.abs(indices[:, None] - indices[None, :])
    factor = jax.random.uniform(key, (length, length), jnp.float32, 0.5, 1.5)
    return jnp.exp(-distance * 4.0 / length) * factor * (2.0 / math.sqrt(length))


def draw_z_kernel(key, part):
    return kernel_draw(jax.random.fold_in(key, 11), NZ)


def draw_x_kernel(key, part):
    return kernel_draw(jax.random.fold_in(key, 23), NX)


def level_of(stream_key, extent, cuts, least, largest):
    loudness, own = 1.0, jax.random.fold_in(stream_key, 6)
    for axis_at, parts in cuts:
        heights = jnp.exp(jax.random.uniform(jax.random.fold_in(own, axis_at), (parts,), jnp.float32, least / len(cuts), largest / len(cuts)))
        loudness = loudness * jnp.repeat(heights, extent[axis_at] // parts).reshape([-1 if axis == axis_at else 1 for axis in range(len(extent))])
    return loudness


def gaussian(stream_key, dims, scale, most, pieces=(), kind=jnp.bfloat16):
    array = scale * jax.random.normal(stream_key, dims, jnp.float32)
    if pieces:
        array = array * level_of(stream_key, dims, pieces, -0.22, 0.18)
    return jnp.clip(array, -most, most).astype(kind)


def setup_inputs(seed: int = 0) -> dict:
    seeds = jax.random.split(jax.random.key(seed), 6)
    image = gaussian(seeds[0], (SUBJECTS, NZ, YW, NX), 1.0, 6.0, ((0, 32), (1, 16)), jnp.float32)
    velocity = gaussian(seeds[1], (SUBJECTS, 3, NZ, YW, NX), 0.5, 3.0, ((0, 32), (2, 16)), jnp.float32)
    template = gaussian(seeds[2], (NZ, YW, NX), 1.0, 6.0, ((0, 16), (1, 32)), jnp.float32)
    z_kernel = draw_z_kernel(jax.random.fold_in(seeds[5], 71), 0)
    x_kernel = draw_x_kernel(jax.random.fold_in(seeds[5], 71), 0)
    return dict(image=image, velocity=velocity, template=template, z_kernel=z_kernel, x_kernel=x_kernel)


def gradients(padded):
    slope_z = (padded[2:, 1:-1, 1:-1] - padded[:-2, 1:-1, 1:-1]) * 0.5
    slope_y = (padded[1:-1, 2:, 1:-1] - padded[1:-1, :-2, 1:-1]) * 0.5
    slope_x = (padded[1:-1, 1:-1, 2:] - padded[1:-1, 1:-1, :-2]) * 0.5
    return jnp.stack([slope_z, slope_y, slope_x])


def reference(image, velocity, template, z_kernel, x_kernel):
    highest = lax.Precision.HIGHEST
    slopes = gradients(jnp.pad(template, 1))

    def per_subject(inputs):
        picture, motion = inputs
        warped = template + jnp.sum(motion * slopes, 0)
        misfit = picture - warped
        forces = misfit[None] * slopes
        along_x = jnp.einsum('czyx,wx->czyw', forces, x_kernel, precision=highest)
        along_z = jnp.einsum('vz,czyw->cvyw', z_kernel, along_x, precision=highest)
        return along_z, misfit

    updates, residuals = lax.map(per_subject, (image, velocity))
    new_template = template + jnp.sum(residuals, 0) / SUBJECTS
    return updates, new_template
```

```python
import jax
import jax.numpy as jnp
from jax import lax
from jax.experimental import pallas as pl
from jax.experimental.pallas import tpu as pltpu
from jax.sharding import Mesh, PartitionSpec as P

ROW = ("y", "x", "c")
COL = ("zl", "zh")
LANES, WIDE = 128, 256


def split_lanes(a):
    return a[..., :LANES], a[..., LANES:]


def template_pieces(row):
    low, high = split_lanes(row)
    return jnp.concatenate([low, jnp.pad(high, ((0, 0), (0, 64)))], 0)


def gather_template(row, raw):
    piece = template_pieces(row)
    by_z = lax.all_to_all(
        jnp.broadcast_to(piece[None], (16, 24, LANES)), COL, 0, 0, tiled=True
    )
    by_z, raw = lax.optimization_barrier((by_z, raw))
    mine = lax.all_to_all(by_z.reshape(8, 2, 24, LANES), ("x", "c"), 0, 0, tiled=True)
    after = [(i, i + 1) for i in range(31)]
    prev = lax.ppermute(mine, ROW, after)
    succ = lax.ppermute(mine, ROW, [(j, i) for i, j in after])
    return prev, mine, succ, raw


def pack_raw(image, velocity):
    four = jnp.concatenate([image[None], velocity], 0)
    low, high = split_lanes(four)
    pairs = jnp.concatenate([high[0::2], high[1::2]], -1)
    six = jnp.concatenate([low, pairs], 0)
    return six.transpose(2, 0, 1, 3).reshape(32, 72, LANES)


def place(refs, half, out):
    for r, ref in enumerate(refs):
        out[r] = jnp.zeros((208, WIDE), jnp.float32)
        for x in range(4):
            for h in range(2):
                for c in range(2):
                    at = 8 + 48 * x + 24 * h + 12 * c
                    out[r, at : at + 12, :LANES] = ref[2 * x + c, h, :12]
                    out[r, at : at + 12, LANES:] = ref[2 * x + c, h, 12:]


def slopes_of(grid, start, rows):
    here = grid[1, pl.ds(start, rows), :]
    sz = (grid[1, pl.ds(start + 1, rows), :] - grid[1, pl.ds(start - 1, rows), :]) * 0.5
    sy = (grid[2, pl.ds(start, rows), :] - grid[0, pl.ds(start, rows), :]) * 0.5
    sx = (pltpu.roll(here, WIDE - 1, 1) - pltpu.roll(here, 1, 1)) * 0.5
    return here, sz, sy, sx


def template_kernel(prev, mine, succ, tmpl, slopes, grid):
    place((prev, mine, succ), None, grid)
    here, sz, sy, sx = slopes_of(grid, 8, 192)
    tmpl[...] = here
    lane = lax.broadcasted_iota(jnp.int32, (192, WIDE), 1)
    slopes[0] = sz
    slopes[1] = sy
    slopes[2] = jnp.where(lane < 192, sx, 0.0)


def template_and_slopes(prev, mine, succ):
    return pl.pallas_call(
        template_kernel,
        out_shape=(
            jax.ShapeDtypeStruct((192, WIDE), jnp.float32),
            jax.ShapeDtypeStruct((3, 192, WIDE), jnp.float32),
        ),
        scratch_shapes=[pltpu.VMEM((3, 208, WIDE), jnp.float32)],
    )(prev, mine, succ)


def halves(a, zh, axis=-2):
    lead = a.shape[:-2]
    b = a.reshape(*lead, 4, 2, 24, a.shape[-1])
    first, second = b[..., 0, :, :], b[..., 1, :, :]
    own = jnp.where(zh == 0, first, second).reshape(*lead, 96, a.shape[-1])
    other = jnp.where(zh == 0, second, first).reshape(*lead, 96, a.shape[-1])
    return own, other


def per_device(image, velocity, template, z_kernel, x_kernel):
    highest = lax.Precision.HIGHEST
    zh = lax.axis_index("zh")
    raw = lax.all_to_all(pack_raw(image[0], velocity[0]), ROW, 0, 0, tiled=True)
    prev, mine, succ, raw = gather_template(template[:, 0, :], raw)
    tmpl, slopes = template_and_slopes(prev, mine, succ)
    own_t, _ = halves(tmpl, zh)
    own_s, other_s = halves(slopes, zh)

    six = raw.reshape(4, 8, 6, 12, LANES).transpose(2, 0, 1, 3, 4).reshape(6, 4, 96, LANES)
    low, pairs = six[:4], six[4:]
    zero = jnp.zeros((4, 4, 96, 64), jnp.float32)
    high = jnp.stack([pairs[0, ..., :64], pairs[0, ..., 64:], pairs[1, ..., :64], pairs[1, ..., 64:]])
    four = jnp.concatenate([low, high, zero], -1)
    residual = four[0] - (own_t + jnp.sum(four[1:] * own_s[:, None], 0))

    sent = jnp.concatenate(
        [
            residual[..., :LANES],
            jnp.concatenate([residual[0::2, :, LANES:192], residual[1::2, :, LANES:192]], -1),
        ],
        0,
    )
    got = lax.ppermute(sent, "zh", [(0, 1), (1, 0)])
    high = jnp.stack([got[4, :, :64], got[4, :, 64:], got[5, :, :64], got[5, :, 64:]])
    other = jnp.concatenate([got[:4], high, zero[0]], -1)

    local = jnp.sum(residual, 0).reshape(8, 12, WIDE)
    local = jnp.concatenate([local[..., :LANES], local[..., LANES:]], 1)
    summed = jnp.sum(lax.all_to_all(local, "zl", 0, 0, tiled=True), 0)
    swap = [
        ((zl * 4 + x) * 2 + c, ((2 * x + c) * 4 + zl // 2) * 2 + zl % 2)
        for zl in range(8)
        for x in range(4)
        for c in range(2)
    ]
    summed = lax.ppermute(summed, ("zl", "x", "c"), swap)
    summed = jnp.concatenate([summed[:12], summed[12:, :64]], -1)
    new_template = template + summed[:, None, :] / 32

    forces = jnp.concatenate(
        [residual[:, None] * own_s[None], other[:, None] * other_s[None]], 2
    )
    k_own, _ = halves(z_kernel, zh)
    k_oo, k_op = halves(k_own.T, zh)
    k = jnp.concatenate([k_oo, k_op], 0)
    along_z = jnp.einsum("zv,sczx->scvx", k, forces[..., :192], precision=highest)
    update = jnp.einsum("scvx,wx->scvw", along_z, x_kernel, precision=highest)
    update = update.reshape(4, 3, 8, 12, 192).transpose(0, 2, 1, 3, 4).reshape(32, 3, 12, 192)
    low, high = split_lanes(update)
    high = jnp.concatenate([high[:, :, :6], high[:, :, 6:]], -1)
    packed = jnp.concatenate([low.reshape(32, 36, LANES), high.reshape(32, 18, LANES)], 1)
    back = lax.all_to_all(packed, ROW, 0, 0, tiled=True)
    low = back[:, :36].reshape(32, 3, 12, LANES)
    high = back[:, 36:].reshape(32, 3, 6, LANES)
    high = jnp.concatenate([high[..., :64], high[..., 64:]], 2)
    out = jnp.concatenate([low, high], -1).transpose(1, 2, 0, 3)
    return out[None], new_template


def solution(mesh):
    fine = Mesh(mesh.devices.reshape(4, 8, 4, 2, 2), ("y", "zl", "x", "zh", "c"))
    subj, slab = ("y", "zl"), ("x", "zh", "c")
    in_specs = (
        P(subj, slab, None, None),
        P(subj, None, slab, None, None),
        P(slab, subj, None),
        P(),
        P(),
    )
    out_specs = (P(subj, None, slab, None, None), P(slab, subj, None))
    return jax.shard_map(
        per_device, mesh=fine, in_specs=in_specs, out_specs=out_specs, check_vma=False
    )
```

```python
import jax
import jax.numpy as jnp
from jax import lax
from jax.experimental import pallas as pl
from jax.experimental.pallas import tpu as pltpu
from jax.sharding import Mesh, PartitionSpec as P

ROW = ("y", "x", "c")
COL = ("zl", "zh")
LANES, WIDE = 128, 256
F32 = jnp.float32
BF16 = jnp.bfloat16


def shape(*dims):
    return jax.ShapeDtypeStruct(dims, F32)


def vmem(n):
    return [pl.BlockSpec(memory_space=pltpu.VMEM)] * n


def smem():
    return pl.BlockSpec(memory_space=pltpu.SMEM)


def call(kernel, outs, scratch=()):
    def run(place, *args):
        return pl.pallas_call(
            kernel,
            out_shape=outs,
            in_specs=[smem(), *vmem(len(args))],
            out_specs=tuple(vmem(len(outs))),
            scratch_shapes=list(scratch),
        )(place, *args)

    return run


def piece_kernel(place, row, out):
    values = row[:, 0, :]
    for i in range(16):
        out[i, :12, :] = values[:, :LANES]
        out[i, 12:, :] = jnp.concatenate([values[:, LANES:], jnp.zeros((12, 64), F32)], 1)


def pack_kernel(place, image, velocity, *outs):
    for s, out in enumerate(outs):
        at = pl.multiple_of(8 * lax.rem(place[0] + s, 4), 8)
        rows = pl.ds(at, 8)
        for a in range(4):
            src = image if a == 0 else velocity.at[a - 1]
            out[a] = src[:, rows, :LANES]
        for k in range(2):
            first = image if k == 0 else velocity.at[1]
            second = velocity.at[2 * k]
            out[4 + k] = jnp.concatenate([first[:, rows, LANES:], second[:, rows, LANES:]], -1)


def residual_kernel(place, tmpl, prev_row, next_row, by_core, by_x, *rest):
    raws, (out, total) = rest[:4], rest[4:]
    zh, c = place[1], place[2]
    low, high = tmpl[zh, :12], tmpl[zh, 12:]
    here = jnp.concatenate([low, high], -1)

    at_x = jnp.logical_and(c == 0, zh == 0)
    z_from = jnp.where(c == 0, 1 - zh, zh)
    before = jnp.where(
        at_x,
        jnp.concatenate([by_x[1, 1], by_x[1, 3]], -1),
        jnp.concatenate([by_core[z_from, 1], by_core[z_from, 3]], -1),
    )
    at_x = jnp.logical_and(c == 1, zh == 1)
    z_from = jnp.where(c == 0, zh, 1 - zh)
    after = jnp.where(
        at_x,
        jnp.concatenate([by_x[0, 0], by_x[0, 2]], -1),
        jnp.concatenate([by_core[z_from, 0], by_core[z_from, 2]], -1),
    )
    up = jnp.concatenate([here[1:], after[None]], 0)
    down = jnp.concatenate([before[None], here[:-1]], 0)
    slope_z = (up - down) * 0.5

    line = lax.broadcasted_iota(jnp.int32, (12, 8, WIDE), 1)

    def edge(ref):
        e = jnp.concatenate([ref[zh, :12], ref[zh, 12:]], -1)
        return jnp.broadcast_to(e[:, None, :], (12, 8, WIDE))

    up = jnp.where(line == 7, edge(next_row), pltpu.roll(here, 7, 1))
    down = jnp.where(line == 0, edge(prev_row), pltpu.roll(here, 1, 1))
    slope_y = (up - down) * 0.5
    slope_x = (pltpu.roll(here, WIDE - 1, 2) - pltpu.roll(here, 1, 2)) * 0.5

    slopes = (slope_z, slope_y, slope_x)
    lane = lax.broadcasted_iota(jnp.int32, (12, 8, LANES), 2)
    sum_low = jnp.zeros((12, 8, LANES), F32)
    sum_high = jnp.zeros((12, 8, LANES), F32)
    highs = []
    for s, raw in enumerate(raws):
        warped = here[..., :LANES]
        motion = raw[1] * slopes[0][..., :LANES] + raw[2] * slopes[1][..., :LANES] + raw[3] * slopes[2][..., :LANES]
        r_low = raw[0] - (warped + motion)
        zero_one, two_three = raw[4], raw[5]
        swap_01, swap_23 = pltpu.roll(zero_one, 64, 2), pltpu.roll(two_three, 64, 2)
        motion = swap_01 * slopes[0][..., LANES:] + two_three * slopes[1][..., LANES:] + swap_23 * slopes[2][..., LANES:]
        r_high = zero_one - (here[..., LANES:] + motion)
        out[12 * s : 12 * s + 12] = r_low
        highs.append(r_high)
        sum_low += r_low
        sum_high += r_high
    for k in range(2):
        out[48 + 12 * k : 60 + 12 * k] = jnp.where(lane < 64, highs[2 * k], pltpu.roll(highs[2 * k + 1], 64, 2))
    total[:12] = sum_low
    total[12:] = sum_high


def main_kernel(place, rows, own, other, zk, xk, out, grid, force, part):
    y, zh = place[0], place[1]
    for r in range(3):
        grid[r] = jnp.zeros((208, WIDE), F32)
        for x in range(4):
            for h in range(2):
                for c in range(2):
                    at = 8 + 48 * x + 24 * h + 12 * c
                    grid[r, at : at + 12, :LANES] = rows[2 * x + c, r, h, :12]
                    grid[r, at : at + 12, LANES:] = rows[2 * x + c, r, h, 12:]
    here = grid[1, 8:200]
    low_lane = lax.broadcasted_iota(jnp.int32, (192, LANES), 1) < 64
    slopes = (
        (grid[1, 9:201] - grid[1, 7:199]) * 0.5,
        (grid[2, 8:200] - grid[0, 8:200]) * 0.5,
        (pltpu.roll(here, WIDE - 1, 1) - pltpu.roll(here, 1, 1)) * 0.5,
    )
    for c, slope in enumerate(slopes):
        high = slope[:, LANES:]
        part[c, :, :LANES] = slope[:, :LANES]
        part[c, :, LANES:] = jnp.where(low_lane, high, pltpu.roll(high, 64, 1))

    for ref, h in ((own, zh), (other, 1 - zh)):
        for x in range(4):
            at = pl.ds(pl.multiple_of(48 * x + 24 * h, 8), 24)
            for b in range(6):
                r = jnp.concatenate([ref[2 * x, 12 * b : 12 * b + 12], ref[2 * x + 1, 12 * b : 12 * b + 12]], 0)
                for c in range(3):
                    s = part[c, at, :LANES] if b < 4 else part[c, at, LANES:]
                    force[at, (c * 6 + b) * LANES : (c * 6 + b + 1) * LANES] = r * s

    def split(a):
        top = a.astype(BF16)
        return top, (a - top.astype(F32)).astype(BF16)

    def times(a, b):
        (a1, a0), (b1, b0) = a, b
        dot = lambda p, q: jnp.dot(p, q, preferred_element_type=F32)
        return dot(a1, b1) + (dot(a1, b0) + dot(a0, b1))

    zrows = jnp.concatenate(
        [zk[pl.ds(pl.multiple_of(48 * x + 24 * zh, 8), 24), :] for x in range(4)], 0
    )
    smooth = times(split(zrows), split(force[...]))

    xt = xk[...]
    zeros = jnp.zeros((64, 192), F32)
    for odd in range(2):
        cols = [xt[:LANES], zeros, xt[LANES:]] if odd else [xt[:LANES], xt[LANES:], zeros]
        weights = split(jnp.concatenate(cols, 0))
        left = []
        for s in (odd, odd + 2):
            for c in range(3):
                at = c * 6 * LANES
                left.append(
                    jnp.concatenate(
                        [
                            smooth[:, at + s * LANES : at + (s + 1) * LANES],
                            smooth[:, at + (4 + s // 2) * LANES : at + (5 + s // 2) * LANES],
                        ],
                        1,
                    )
                )
        update = times(split(jnp.concatenate(left, 0)), weights)
        for i, s in enumerate((odd, odd + 2)):
            to = 8 * lax.rem(y + 4 - s, 4)
            for c in range(3):
                for j in range(8):
                    at = (i * 3 + c) * 96 + 12 * j
                    piece = update[at : at + 12]
                    out[to + j, 12 * c : 12 * c + 12, :] = piece[:, :LANES]
                    out[to + j, 36 + 6 * c : 42 + 6 * c, :] = jnp.concatenate(
                        [piece[:6, LANES:], piece[6:, LANES:]], 1
                    )


def per_device(image, velocity, template, z_kernel, x_kernel):
    place = jnp.stack([lax.axis_index(a) for a in ("y", "zh", "c")]).astype(jnp.int32)

    (piece,) = call(piece_kernel, (shape(16, 24, LANES),))(place, template)
    gathered = lax.all_to_all(piece, COL, 0, 0, tiled=True).reshape(8, 2, 24, LANES)

    raws = call(pack_kernel, (shape(6, 12, 8, LANES),) * 4)(place, image[0], velocity[0])
    raws = [raws[0]] + [
        lax.ppermute(raws[s], "y", [(i, (i + s) % 4) for i in range(4)]) for s in (1, 2, 3)
    ]

    prev_row = lax.ppermute(gathered[7], "y", [(i, i + 1) for i in range(3)])
    next_row = lax.ppermute(gathered[0], "y", [(i + 1, i) for i in range(3)])
    ends = jnp.stack([gathered[:, :, i] for i in (0, 11, 12, 23)], 2).transpose(1, 2, 0, 3)
    by_core = lax.ppermute(ends, "c", [(0, 1), (1, 0)])
    by_x = lax.ppermute(ends, ("x", "c"), [(2 * i + 1, 2 * i + 2) for i in range(3)] + [(2 * i + 2, 2 * i + 1) for i in range(3)])
    tmpl = gathered.transpose(1, 2, 0, 3)

    residual, total = call(residual_kernel, (shape(72, 8, LANES), shape(24, 8, LANES)))(
        place, tmpl, prev_row, next_row, by_core, by_x, *raws
    )
    own = lax.all_to_all(residual.transpose(1, 0, 2), ("x", "c"), 0, 0, tiled=True)
    other = lax.ppermute(own, "zh", [(0, 1), (1, 0)])

    summed = lax.psum_scatter(total, "zl", scatter_dimension=1, tiled=True)
    summed = jnp.concatenate([summed[:12], summed[12:, :, :64]], -1)
    new_template = template + summed / 32

    ten = jnp.concatenate([prev_row[None], gathered, next_row[None]], 0)
    rows = jnp.stack([ten[i : i + 8] for i in range(3)], 1)
    rows = lax.all_to_all(rows, ("x", "c"), 0, 0, tiled=True)

    (packed,) = call(
        main_kernel,
        (shape(32, 54, LANES),),
        (
            pltpu.VMEM((3, 208, WIDE), F32),
            pltpu.VMEM((192, 18 * LANES), F32),
            pltpu.VMEM((3, 192, WIDE), F32),
        ),
    )(place, rows, own, other, z_kernel, x_kernel.T)
    back = lax.all_to_all(packed, ROW, 0, 0, tiled=True)
    low = back[:, :36].reshape(32, 3, 12, LANES)
    high = back[:, 36:].reshape(32, 3, 6, LANES)
    high = jnp.concatenate([high[..., :64], high[..., 64:]], 2)
    out = jnp.concatenate([low, high], -1).transpose(1, 2, 0, 3)
    return out[None], new_template


def solution(mesh):
    fine = Mesh(mesh.devices.reshape(4, 8, 4, 2, 2), ("y", "zl", "x", "zh", "c"))
    subj, slab = ("y", "zl"), ("x", "zh", "c")
    in_specs = (
        P(subj, slab, None, None),
        P(subj, None, slab, None, None),
        P(slab, subj, None),
        P(),
        P(),
    )
    out_specs = (P(subj, None, slab, None, None), P(slab, subj, None))
    return jax.shard_map(
        per_device, mesh=fine, in_specs=in_specs, out_specs=out_specs, check_vma=False
    )
```

```python
import jax
import jax.numpy as jnp
from jax import lax
from jax.experimental import pallas as pl
from jax.experimental.pallas import tpu as pltpu
from jax.sharding import Mesh, PartitionSpec as P

ROW = ("y", "x", "c")
COL = ("zl", "zh")
LANES, WIDE = 128, 256
F32 = jnp.float32
BF16 = jnp.bfloat16


def shape(*dims):
    return jax.ShapeDtypeStruct(dims, F32)


def vmem(n):
    return [pl.BlockSpec(memory_space=pltpu.VMEM)] * n


def smem():
    return pl.BlockSpec(memory_space=pltpu.SMEM)


def call(kernel, outs, scratch=()):
    def run(place, *args):
        return pl.pallas_call(
            kernel,
            out_shape=outs,
            in_specs=[smem(), *vmem(len(args))],
            out_specs=tuple(vmem(len(outs))),
            scratch_shapes=list(scratch),
        )(place, *args)

    return run


def piece_kernel(place, row, out):
    values = row[:, 0, :]
    for i in range(16):
        out[i, :12, :] = values[:, :LANES]
        out[i, 12:, :] = jnp.concatenate([values[:, LANES:], jnp.zeros((12, 64), F32)], 1)


def pack_kernel(place, image, velocity, *outs):
    for s, out in enumerate(outs):
        at = pl.multiple_of(8 * lax.rem(place[0] + s, 4), 8)
        rows = pl.ds(at, 8)
        for a in range(4):
            src = image if a == 0 else velocity.at[a - 1]
            out[a] = src[:, rows, :LANES]
        for k in range(2):
            first = image if k == 0 else velocity.at[1]
            second = velocity.at[2 * k]
            out[4 + k] = jnp.concatenate([first[:, rows, LANES:], second[:, rows, LANES:]], -1)


def residual_kernel(place, tmpl, prev_row, next_row, by_core, by_x, *rest):
    raws, (out, total) = rest[:4], rest[4:]
    zh, c = place[1], place[2]
    low, high = tmpl[zh, :12], tmpl[zh, 12:]
    here = jnp.concatenate([low, high], -1)

    at_x = jnp.logical_and(c == 0, zh == 0)
    z_from = jnp.where(c == 0, 1 - zh, zh)
    before = jnp.where(
        at_x,
        jnp.concatenate([by_x[1, 1], by_x[1, 3]], -1),
        jnp.concatenate([by_core[z_from, 1], by_core[z_from, 3]], -1),
    )
    at_x = jnp.logical_and(c == 1, zh == 1)
    z_from = jnp.where(c == 0, zh, 1 - zh)
    after = jnp.where(
        at_x,
        jnp.concatenate([by_x[0, 0], by_x[0, 2]], -1),
        jnp.concatenate([by_core[z_from, 0], by_core[z_from, 2]], -1),
    )
    up = jnp.concatenate([here[1:], after[None]], 0)
    down = jnp.concatenate([before[None], here[:-1]], 0)
    slope_z = (up - down) * 0.5

    line = lax.broadcasted_iota(jnp.int32, (12, 8, WIDE), 1)

    def edge(ref):
        e = jnp.concatenate([ref[zh, :12], ref[zh, 12:]], -1)
        return jnp.broadcast_to(e[:, None, :], (12, 8, WIDE))

    up = jnp.where(line == 7, edge(next_row), pltpu.roll(here, 7, 1))
    down = jnp.where(line == 0, edge(prev_row), pltpu.roll(here, 1, 1))
    slope_y = (up - down) * 0.5
    slope_x = (pltpu.roll(here, WIDE - 1, 2) - pltpu.roll(here, 1, 2)) * 0.5

    slopes = (slope_z, slope_y, slope_x)
    lane = lax.broadcasted_iota(jnp.int32, (12, 8, LANES), 2)
    sum_low = jnp.zeros((12, 8, LANES), F32)
    sum_high = jnp.zeros((12, 8, LANES), F32)
    highs = []
    for s, raw in enumerate(raws):
        warped = here[..., :LANES]
        motion = raw[1] * slopes[0][..., :LANES] + raw[2] * slopes[1][..., :LANES] + raw[3] * slopes[2][..., :LANES]
        r_low = raw[0] - (warped + motion)
        zero_one, two_three = raw[4], raw[5]
        swap_01, swap_23 = pltpu.roll(zero_one, 64, 2), pltpu.roll(two_three, 64, 2)
        motion = swap_01 * slopes[0][..., LANES:] + two_three * slopes[1][..., LANES:] + swap_23 * slopes[2][..., LANES:]
        r_high = zero_one - (here[..., LANES:] + motion)
        out[12 * s : 12 * s + 12] = r_low
        highs.append(r_high)
        sum_low += r_low
        sum_high += r_high
    for k in range(2):
        out[48 + 12 * k : 60 + 12 * k] = jnp.where(lane < 64, highs[2 * k], pltpu.roll(highs[2 * k + 1], 64, 2))
    total[:12] = sum_low
    total[12:] = sum_high


def main_kernel(place, prev, mine, succ, got, zk, xk, out, grid, force):
    y, zh = place[0], place[1]
    for r, ref in enumerate((prev, mine, succ)):
        grid[r, :8] = jnp.zeros((8, WIDE), F32)
        grid[r, 200:] = jnp.zeros((8, WIDE), F32)
        for x in range(4):
            for h in range(2):
                for c in range(2):
                    at = 8 + 48 * x + 24 * h + 12 * c
                    grid[r, at : at + 12, :LANES] = ref[2 * x + c, h, :12]
                    grid[r, at : at + 12, LANES:] = ref[2 * x + c, h, 12:]
    here = grid[1, 8:200]
    low_lane = lax.broadcasted_iota(jnp.int32, (192, LANES), 1) < 64
    slopes = (
        (grid[1, 9:201] - grid[1, 7:199]) * 0.5,
        (grid[2, 8:200] - grid[0, 8:200]) * 0.5,
        (pltpu.roll(here, WIDE - 1, 1) - pltpu.roll(here, 1, 1)) * 0.5,
    )
    slopes = [(a[:, :LANES], jnp.where(low_lane, a[:, LANES:], pltpu.roll(a[:, LANES:], 64, 1))) for a in slopes]
    for k in range(8):
        at = slice(24 * k, 24 * k + 24)
        for b in range(6):
            r = jnp.concatenate([got[2 * k, 12 * b : 12 * b + 12], got[2 * k + 1, 12 * b : 12 * b + 12]], 0)
            for c in range(3):
                force[at, (c * 6 + b) * LANES : (c * 6 + b + 1) * LANES] = r * slopes[c][b // 4][at]

    def split(a):
        top = a.astype(BF16)
        return top, (a - top.astype(F32)).astype(BF16)

    def times(a, b):
        (a1, a0), (b1, b0) = a, b
        dot = lambda p, q: jnp.dot(p, q, preferred_element_type=F32)
        return dot(a1, b1) + (dot(a1, b0) + dot(a0, b1))

    zrows = jnp.concatenate(
        [zk[pl.ds(pl.multiple_of(48 * x + 24 * zh, 8), 24), :] for x in range(4)], 0
    )
    smooth = times(split(zrows), split(force[...]))

    xt = xk[...]
    zeros = jnp.zeros((64, 192), F32)
    for odd in range(2):
        cols = [xt[:LANES], zeros, xt[LANES:]] if odd else [xt[:LANES], xt[LANES:], zeros]
        weights = split(jnp.concatenate(cols, 0))
        left = []
        for s in (odd, odd + 2):
            for c in range(3):
                at = c * 6 * LANES
                left.append(
                    jnp.concatenate(
                        [
                            smooth[:, at + s * LANES : at + (s + 1) * LANES],
                            smooth[:, at + (4 + s // 2) * LANES : at + (5 + s // 2) * LANES],
                        ],
                        1,
                    )
                )
        update = times(split(jnp.concatenate(left, 0)), weights)
        for i, s in enumerate((odd, odd + 2)):
            to = 8 * lax.rem(y + 4 - s, 4)
            for c in range(3):
                for j in range(8):
                    at = (i * 3 + c) * 96 + 12 * j
                    piece = update[at : at + 12]
                    out[to + j, 12 * c : 12 * c + 12, :] = piece[:, :LANES]
                    out[to + j, 36 + 6 * c : 42 + 6 * c, :] = jnp.concatenate(
                        [piece[:6, LANES:], piece[6:, LANES:]], 1
                    )


def per_device(image, velocity, template, z_kernel, x_kernel):
    place = jnp.stack([lax.axis_index(a) for a in ("y", "zh", "c")]).astype(jnp.int32)

    (piece,) = call(piece_kernel, (shape(16, 24, LANES),))(place, template)
    gathered = lax.all_to_all(piece, COL, 0, 0, tiled=True).reshape(8, 2, 24, LANES)

    raws = call(pack_kernel, (shape(6, 12, 8, LANES),) * 4)(place, image[0], velocity[0])
    raws = [raws[0]] + [
        lax.ppermute(raws[s], "y", [(i, (i + s) % 4) for i in range(4)]) for s in (1, 2, 3)
    ]

    prev_row = lax.ppermute(gathered[7], "y", [(i, i + 1) for i in range(3)])
    next_row = lax.ppermute(gathered[0], "y", [(i + 1, i) for i in range(3)])
    ends = jnp.stack([gathered[:, :, i] for i in (0, 11, 12, 23)], 2).transpose(1, 2, 0, 3)
    by_core = lax.ppermute(ends, "c", [(0, 1), (1, 0)])
    by_x = lax.ppermute(ends, ("x", "c"), [(2 * i + 1, 2 * i + 2) for i in range(3)] + [(2 * i + 2, 2 * i + 1) for i in range(3)])
    tmpl = gathered.transpose(1, 2, 0, 3)
    mine = lax.all_to_all(gathered, ("x", "c"), 0, 0, tiled=True)

    residual, total = call(residual_kernel, (shape(72, 8, LANES), shape(24, 8, LANES)))(
        place, tmpl, prev_row, next_row, by_core, by_x, *raws
    )
    residual, mine = lax.optimization_barrier((residual, mine))
    by_row = residual.transpose(1, 0, 2).reshape(4, 1, 2, 72, LANES)
    by_row = jnp.broadcast_to(by_row, (4, 2, 2, 72, LANES)).reshape(16, 72, LANES)
    got = lax.all_to_all(by_row, ("x", "zh", "c"), 0, 0, tiled=True)
    along = [(i, i + 1) for i in range(31)]
    prev = lax.ppermute(mine, ROW, along)
    succ = lax.ppermute(mine, ROW, [(j, i) for i, j in along])

    total, zl = total.transpose(1, 0, 2), lax.axis_index("zl")
    for step in (4, 2, 1):
        high = (zl // step) % 2
        keep = lax.dynamic_slice_in_dim(total, high * step, step)
        give = lax.dynamic_slice_in_dim(total, (1 - high) * step, step)
        total = keep + lax.ppermute(give, "zl", [(i, i ^ step) for i in range(8)])
    total = total[0]
    summed = jnp.concatenate([total[:12], total[12:, :64]], -1)[:, None]
    new_template = template + summed / 32

    (packed,) = call(
        main_kernel,
        (shape(32, 54, LANES),),
        (pltpu.VMEM((3, 208, WIDE), F32), pltpu.VMEM((192, 18 * LANES), F32)),
    )(place, prev, mine, succ, got, z_kernel, x_kernel.T)
    back = lax.all_to_all(packed, ROW, 0, 0, tiled=True)
    low = back[:, :36].reshape(32, 3, 12, LANES)
    high = back[:, 36:].reshape(32, 3, 6, LANES)
    high = jnp.concatenate([high[..., :64], high[..., 64:]], 2)
    out = jnp.concatenate([low, high], -1).transpose(1, 2, 0, 3)
    return out[None], new_template


def solution(mesh):
    fine = Mesh(mesh.devices.reshape(4, 8, 4, 2, 2), ("y", "zl", "x", "zh", "c"))
    subj, slab = ("y", "zl"), ("x", "zh", "c")
    in_specs = (
        P(subj, slab, None, None),
        P(subj, None, slab, None, None),
        P(slab, subj, None),
        P(),
        P(),
    )
    out_specs = (P(subj, None, slab, None, None), P(slab, subj, None))
    return jax.shard_map(
        per_device, mesh=fine, in_specs=in_specs, out_specs=out_specs, check_vma=False
    )
```

```python
import jax
import jax.numpy as jnp
from jax import lax
from jax.experimental import pallas as pl
from jax.experimental.pallas import tpu as pltpu
from jax.sharding import Mesh, PartitionSpec as P

ROW = ("y", "x", "c")
COL = ("zl", "zh")
LANES, WIDE = 128, 256
F32 = jnp.float32
BF16 = jnp.bfloat16


def shape(*dims):
    return jax.ShapeDtypeStruct(dims, F32)


def vmem(n):
    return [pl.BlockSpec(memory_space=pltpu.VMEM)] * n


def smem():
    return pl.BlockSpec(memory_space=pltpu.SMEM)


def call(kernel, outs, scratch=()):
    def run(place, *args):
        return pl.pallas_call(
            kernel,
            out_shape=outs,
            in_specs=[smem(), *vmem(len(args))],
            out_specs=tuple(vmem(len(outs))),
            scratch_shapes=list(scratch),
        )(place, *args)

    return run


def piece_kernel(place, row, out):
    values = row[:, 0, :]
    for i in range(16):
        out[i, :12, :] = values[:, :LANES]
        out[i, 12:, :] = jnp.concatenate([values[:, LANES:], jnp.zeros((12, 64), F32)], 1)


def pack_kernel(place, image, velocity, *outs):
    for s, out in enumerate(outs):
        at = pl.multiple_of(8 * lax.rem(place[0] + s, 4), 8)
        rows = pl.ds(at, 8)
        for a in range(4):
            src = image if a == 0 else velocity.at[a - 1]
            out[a] = src[:, rows, :LANES]
        for k in range(2):
            first = image if k == 0 else velocity.at[1]
            second = velocity.at[2 * k]
            out[4 + k] = jnp.concatenate([first[:, rows, LANES:], second[:, rows, LANES:]], -1)


def halo_kernel(place, gathered, tmpl, ends, first, last):
    for h in range(2):
        for k in range(3):
            block = jnp.swapaxes(gathered[:, h, 8 * k : 8 * k + 8], 0, 1)
            tmpl[h, 8 * k : 8 * k + 8] = block
            for i, p in enumerate((0, 11, 12, 23)):
                if p // 8 == k:
                    ends[h, i] = block[p % 8]
        first[h] = gathered[0, h]
        last[h] = gathered[7, h]


def residual_kernel(place, tmpl, prev_row, next_row, by_core, by_x, *rest):
    raws, out, parts, (rows, total) = rest[:4], rest[4], rest[5:9], rest[9:]
    zh, c, zl = place[1], place[2], place[3]
    low, high = tmpl[zh, :12], tmpl[zh, 12:]
    here = jnp.concatenate([low, high], -1)

    at_x = jnp.logical_and(c == 0, zh == 0)
    z_from = jnp.where(c == 0, 1 - zh, zh)
    before = jnp.where(
        at_x,
        jnp.concatenate([by_x[1, 1], by_x[1, 3]], -1),
        jnp.concatenate([by_core[z_from, 1], by_core[z_from, 3]], -1),
    )
    at_x = jnp.logical_and(c == 1, zh == 1)
    z_from = jnp.where(c == 0, zh, 1 - zh)
    after = jnp.where(
        at_x,
        jnp.concatenate([by_x[0, 0], by_x[0, 2]], -1),
        jnp.concatenate([by_core[z_from, 0], by_core[z_from, 2]], -1),
    )
    up = jnp.concatenate([here[1:], after[None]], 0)
    down = jnp.concatenate([before[None], here[:-1]], 0)
    slope_z = (up - down) * 0.5

    line = lax.broadcasted_iota(jnp.int32, (12, 8, WIDE), 1)

    def edge(ref):
        e = jnp.concatenate([ref[zh, :12], ref[zh, 12:]], -1)
        return jnp.broadcast_to(e[:, None, :], (12, 8, WIDE))

    up = jnp.where(line == 7, edge(next_row), pltpu.roll(here, 7, 1))
    down = jnp.where(line == 0, edge(prev_row), pltpu.roll(here, 1, 1))
    slope_y = (up - down) * 0.5
    slope_x = (pltpu.roll(here, WIDE - 1, 2) - pltpu.roll(here, 1, 2)) * 0.5

    slopes = (slope_z, slope_y, slope_x)
    lane = lax.broadcasted_iota(jnp.int32, (12, 8, LANES), 2)
    sum_low = jnp.zeros((12, 8, LANES), F32)
    sum_high = jnp.zeros((12, 8, LANES), F32)
    highs = []
    for s, raw in enumerate(raws):
        warped = here[..., :LANES]
        motion = raw[1] * slopes[0][..., :LANES] + raw[2] * slopes[1][..., :LANES] + raw[3] * slopes[2][..., :LANES]
        r_low = raw[0] - (warped + motion)
        zero_one, two_three = raw[4], raw[5]
        swap_01, swap_23 = pltpu.roll(zero_one, 64, 2), pltpu.roll(two_three, 64, 2)
        motion = swap_01 * slopes[0][..., LANES:] + two_three * slopes[1][..., LANES:] + swap_23 * slopes[2][..., LANES:]
        r_high = zero_one - (here[..., LANES:] + motion)
        rows[12 * s : 12 * s + 12] = r_low
        highs.append(r_high)
        sum_low += r_low
        sum_high += r_high
    for k in range(2):
        rows[48 + 12 * k : 60 + 12 * k] = jnp.where(lane < 64, highs[2 * k], pltpu.roll(highs[2 * k + 1], 64, 2))
    rows[72:84] = sum_low
    rows[84:] = sum_high
    for k in range(12):
        block = jnp.swapaxes(rows[8 * k : 8 * k + 8], 0, 1)
        if k >= 9:
            total[:, 8 * (k - 9) : 8 * (k - 8)] = block
            continue
        for i in range(8):
            x, core = i // 2, i % 2
            for h in range(2):
                out[4 * x + 2 * h + core, 8 * k : 8 * k + 8] = block[i]
    for t, part in enumerate(parts):
        part[...] = total[pl.ds(2 * lax.bitwise_xor(zl // 2, t), 2)]


def main_kernel(place, prev, mine, succ, got, zk, xk, *rest):
    parts, (out, keep, give, grid, force) = rest[:4], rest[4:]
    y, zh, odd_row = place[0], place[1], lax.rem(place[3], 2)
    for ref, i in ((keep, odd_row), (give, 1 - odd_row)):
        ref[...] = parts[0][i] + parts[1][i] + parts[2][i] + parts[3][i]
    for r, ref in enumerate((prev, mine, succ)):
        grid[r, :8] = jnp.zeros((8, WIDE), F32)
        grid[r, 200:] = jnp.zeros((8, WIDE), F32)
        for x in range(4):
            for h in range(2):
                for c in range(2):
                    at = 8 + 48 * x + 24 * h + 12 * c
                    grid[r, at : at + 12, :LANES] = ref[2 * x + c, h, :12]
                    grid[r, at : at + 12, LANES:] = ref[2 * x + c, h, 12:]
    here = grid[1, 8:200]
    low_lane = lax.broadcasted_iota(jnp.int32, (192, LANES), 1) < 64
    slopes = (
        (grid[1, 9:201] - grid[1, 7:199]) * 0.5,
        (grid[2, 8:200] - grid[0, 8:200]) * 0.5,
        (pltpu.roll(here, WIDE - 1, 1) - pltpu.roll(here, 1, 1)) * 0.5,
    )
    slopes = [(a[:, :LANES], jnp.where(low_lane, a[:, LANES:], pltpu.roll(a[:, LANES:], 64, 1))) for a in slopes]
    for k in range(8):
        at = slice(24 * k, 24 * k + 24)
        for b in range(6):
            r = jnp.concatenate([got[2 * k, 12 * b : 12 * b + 12], got[2 * k + 1, 12 * b : 12 * b + 12]], 0)
            for c in range(3):
                force[at, (c * 6 + b) * LANES : (c * 6 + b + 1) * LANES] = r * slopes[c][b // 4][at]

    def split(a):
        top = a.astype(BF16)
        return top, (a - top.astype(F32)).astype(BF16)

    def times(a, b):
        (a1, a0), (b1, b0) = a, b
        dot = lambda p, q: jnp.dot(p, q, preferred_element_type=F32)
        return dot(a1, b1) + (dot(a1, b0) + dot(a0, b1))

    zrows = jnp.concatenate(
        [zk[pl.ds(pl.multiple_of(48 * x + 24 * zh, 8), 24), :] for x in range(4)], 0
    )
    smooth = times(split(zrows), split(force[...]))

    xt = xk[...]
    zeros = jnp.zeros((64, 192), F32)
    for odd in range(2):
        cols = [xt[:LANES], zeros, xt[LANES:]] if odd else [xt[:LANES], xt[LANES:], zeros]
        weights = split(jnp.concatenate(cols, 0))
        left = []
        for s in (odd, odd + 2):
            for c in range(3):
                at = c * 6 * LANES
                left.append(
                    jnp.concatenate(
                        [
                            smooth[:, at + s * LANES : at + (s + 1) * LANES],
                            smooth[:, at + (4 + s // 2) * LANES : at + (5 + s // 2) * LANES],
                        ],
                        1,
                    )
                )
        update = times(split(jnp.concatenate(left, 0)), weights)
        for i, s in enumerate((odd, odd + 2)):
            to = 8 * lax.rem(y + 4 - s, 4)
            for c in range(3):
                for j in range(8):
                    at = (i * 3 + c) * 96 + 12 * j
                    piece = update[at : at + 12]
                    out[to + j, 12 * c : 12 * c + 12, :] = piece[:, :LANES]
                    out[to + j, 36 + 6 * c : 42 + 6 * c, :] = jnp.concatenate(
                        [piece[:6, LANES:], piece[6:, LANES:]], 1
                    )


def per_device(image, velocity, template, z_kernel, x_kernel):
    place = jnp.stack([lax.axis_index(a) for a in ("y", "zh", "c", "zl")]).astype(jnp.int32)

    (piece,) = call(piece_kernel, (shape(16, 24, LANES),))(place, template)
    gathered = lax.all_to_all(piece, COL, 0, 0, tiled=True).reshape(8, 2, 24, LANES)

    raws = call(pack_kernel, (shape(6, 12, 8, LANES),) * 4)(place, image[0], velocity[0])
    raws = [raws[0]] + [
        lax.ppermute(raws[s], "y", [(i, (i + s) % 4) for i in range(4)]) for s in (1, 2, 3)
    ]

    tmpl, ends, first, last = call(
        halo_kernel,
        (shape(2, 24, 8, LANES), shape(2, 4, 8, LANES), shape(2, 24, LANES), shape(2, 24, LANES)),
    )(place, gathered)
    by_core = lax.ppermute(ends, "c", [(0, 1), (1, 0)])
    by_x = lax.ppermute(ends, ("x", "c"), [(2 * i + 1, 2 * i + 2) for i in range(3)] + [(2 * i + 2, 2 * i + 1) for i in range(3)])
    prev_row = lax.ppermute(last, "y", [(i, i + 1) for i in range(3)])
    next_row = lax.ppermute(first, "y", [(i + 1, i) for i in range(3)])
    gathered, by_core = lax.optimization_barrier((gathered, by_core))
    mine = lax.all_to_all(gathered, ("x", "c"), 0, 0, tiled=True)

    by_row, *parts = call(
        residual_kernel,
        (shape(16, 72, LANES), *[shape(2, 24, LANES)] * 4),
        (pltpu.VMEM((96, 8, LANES), F32), pltpu.VMEM((8, 24, LANES), F32)),
    )(place, tmpl, prev_row, next_row, by_core, by_x, *raws)
    by_row, mine = lax.optimization_barrier((by_row, mine))
    got = lax.all_to_all(by_row, ("x", "zh", "c"), 0, 0, tiled=True)
    along = [(i, i + 1) for i in range(31)]
    prev = lax.ppermute(mine, ROW, along)
    succ = lax.ppermute(mine, ROW, [(j, i) for i, j in along])

    for t in (1, 2, 3):
        parts[t] = lax.ppermute(parts[t], "zl", [(i, i ^ (2 * t)) for i in range(8)])

    packed, keep, give = call(
        main_kernel,
        (shape(32, 54, LANES), shape(24, LANES), shape(24, LANES)),
        (pltpu.VMEM((3, 208, WIDE), F32), pltpu.VMEM((192, 18 * LANES), F32)),
    )(place, prev, mine, succ, got, z_kernel, x_kernel.T, *parts)
    total = keep + lax.ppermute(give, "zl", [(i, i ^ 1) for i in range(8)])
    summed = jnp.concatenate([total[:12], total[12:, :64]], -1)[:, None]
    new_template = template + summed / 32

    back = lax.all_to_all(packed, ROW, 0, 0, tiled=True)
    low = back[:, :36].reshape(32, 3, 12, LANES)
    high = back[:, 36:].reshape(32, 3, 6, LANES)
    high = jnp.concatenate([high[..., :64], high[..., 64:]], 2)
    out = jnp.concatenate([low, high], -1).transpose(1, 2, 0, 3)
    return out[None], new_template


def solution(mesh):
    fine = Mesh(mesh.devices.reshape(4, 8, 4, 2, 2), ("y", "zl", "x", "zh", "c"))
    subj, slab = ("y", "zl"), ("x", "zh", "c")
    in_specs = (
        P(subj, slab, None, None),
        P(subj, None, slab, None, None),
        P(slab, subj, None),
        P(),
        P(),
    )
    out_specs = (P(subj, None, slab, None, None), P(slab, subj, None))
    return jax.shard_map(
        per_device, mesh=fine, in_specs=in_specs, out_specs=out_specs, check_vma=False
    )
```

```python
import jax
import jax.numpy as jnp
from jax import lax
from jax.experimental import pallas as pl
from jax.experimental.pallas import tpu as pltpu
from jax.sharding import Mesh, PartitionSpec as P

ROW = ("y", "x", "c")
COL = ("zl", "zh")
LANES, WIDE = 128, 256
F32 = jnp.float32
BF16 = jnp.bfloat16


def shape(*dims):
    return jax.ShapeDtypeStruct(dims, F32)


def vmem(n):
    return [pl.BlockSpec(memory_space=pltpu.VMEM)] * n


def smem():
    return pl.BlockSpec(memory_space=pltpu.SMEM)


def call(kernel, outs, scratch=()):
    def run(place, *args):
        args = [pltpu.with_memory_space_constraint(a, pltpu.VMEM) for a in args]
        first = [] if place is None else [place]
        return pl.pallas_call(
            kernel,
            out_shape=outs,
            in_specs=[*([smem()] * len(first)), *vmem(len(args))],
            out_specs=tuple(vmem(len(outs))),
            scratch_shapes=list(scratch),
        )(*first, *args)

    return run


def piece_kernel(row, out):
    values = row[:, 0, :]
    for i in range(16):
        out[i, :12, :] = values[:, :LANES]
        out[i, 12:, :] = jnp.concatenate([values[:, LANES:], jnp.zeros((12, 64), F32)], 1)


def split(a):
    top = a.astype(BF16)
    return top, (a - top.astype(F32)).astype(BF16)


def pack_kernel(place, image, velocity, zk, xk, *rest):
    outs, (zw, xw) = rest[:4], rest[4:]
    zrows = [zk[pl.ds(pl.multiple_of(48 * x + 24 * place[1], 8), 24), :] for x in range(4)]
    zw[0], zw[1] = split(jnp.concatenate(zrows, 0))
    xt = xk[...].T
    zeros = jnp.zeros((64, 192), F32)
    for odd in range(2):
        cols = [xt[:LANES], zeros, xt[LANES:]] if odd else [xt[:LANES], xt[LANES:], zeros]
        xw[odd, 0], xw[odd, 1] = split(jnp.concatenate(cols, 0))
    for s, out in enumerate(outs):
        at = pl.multiple_of(8 * lax.rem(place[0] + s, 4), 8)
        rows = pl.ds(at, 8)
        for a in range(4):
            src = image if a == 0 else velocity.at[a - 1]
            out[a] = src[:, rows, :LANES]
        for k in range(2):
            first = image if k == 0 else velocity.at[1]
            second = velocity.at[2 * k]
            out[4 + k] = jnp.concatenate([first[:, rows, LANES:], second[:, rows, LANES:]], -1)


def halo_kernel(place, gathered, tmpl, ends, first, last):
    for h in range(2):
        for k in range(3):
            block = jnp.swapaxes(gathered[:, h, 8 * k : 8 * k + 8], 0, 1)
            tmpl[h, 8 * k : 8 * k + 8] = block
            for i, p in enumerate((0, 11, 12, 23)):
                if p // 8 == k:
                    ends[h, i] = block[p % 8]
        first[h] = gathered[0, h]
        last[h] = gathered[7, h]


def residual_kernel(place, tmpl, prev_row, next_row, by_core, by_x, *rest):
    raws, out, parts, (rows, total) = rest[:4], rest[4], rest[5:9], rest[9:]
    zh, c, zl = place[1], place[2], place[3]
    low, high = tmpl[zh, :12], tmpl[zh, 12:]
    here = jnp.concatenate([low, high], -1)

    at_x = jnp.logical_and(c == 0, zh == 0)
    z_from = jnp.where(c == 0, 1 - zh, zh)
    before = jnp.where(
        at_x,
        jnp.concatenate([by_x[1, 1], by_x[1, 3]], -1),
        jnp.concatenate([by_core[z_from, 1], by_core[z_from, 3]], -1),
    )
    at_x = jnp.logical_and(c == 1, zh == 1)
    z_from = jnp.where(c == 0, zh, 1 - zh)
    after = jnp.where(
        at_x,
        jnp.concatenate([by_x[0, 0], by_x[0, 2]], -1),
        jnp.concatenate([by_core[z_from, 0], by_core[z_from, 2]], -1),
    )
    up = jnp.concatenate([here[1:], after[None]], 0)
    down = jnp.concatenate([before[None], here[:-1]], 0)
    slope_z = (up - down) * 0.5

    line = lax.broadcasted_iota(jnp.int32, (12, 8, WIDE), 1)

    def edge(ref):
        e = jnp.concatenate([ref[zh, :12], ref[zh, 12:]], -1)
        return jnp.broadcast_to(e[:, None, :], (12, 8, WIDE))

    up = jnp.where(line == 7, edge(next_row), pltpu.roll(here, 7, 1))
    down = jnp.where(line == 0, edge(prev_row), pltpu.roll(here, 1, 1))
    slope_y = (up - down) * 0.5
    slope_x = (pltpu.roll(here, WIDE - 1, 2) - pltpu.roll(here, 1, 2)) * 0.5

    slopes = (slope_z, slope_y, slope_x)
    lane = lax.broadcasted_iota(jnp.int32, (12, 8, LANES), 2)
    sum_low = jnp.zeros((12, 8, LANES), F32)
    sum_high = jnp.zeros((12, 8, LANES), F32)
    highs = []
    for s, raw in enumerate(raws):
        warped = here[..., :LANES]
        motion = raw[1] * slopes[0][..., :LANES] + raw[2] * slopes[1][..., :LANES] + raw[3] * slopes[2][..., :LANES]
        r_low = raw[0] - (warped + motion)
        zero_one, two_three = raw[4], raw[5]
        swap_01, swap_23 = pltpu.roll(zero_one, 64, 2), pltpu.roll(two_three, 64, 2)
        motion = swap_01 * slopes[0][..., LANES:] + two_three * slopes[1][..., LANES:] + swap_23 * slopes[2][..., LANES:]
        r_high = zero_one - (here[..., LANES:] + motion)
        rows[12 * s : 12 * s + 12] = r_low
        highs.append(r_high)
        sum_low += r_low
        sum_high += r_high
    for k in range(2):
        rows[48 + 12 * k : 60 + 12 * k] = jnp.where(lane < 64, highs[2 * k], pltpu.roll(highs[2 * k + 1], 64, 2))
    rows[72:84] = sum_low
    rows[84:] = sum_high
    for k in range(12):
        block = jnp.swapaxes(rows[8 * k : 8 * k + 8], 0, 1)
        if k >= 9:
            total[:, 8 * (k - 9) : 8 * (k - 8)] = block
            continue
        for i in range(8):
            x, core = i // 2, i % 2
            for h in range(2):
                out[4 * x + 2 * h + core, 8 * k : 8 * k + 8] = block[i]
    for t, part in enumerate(parts):
        part[...] = total[pl.ds(2 * lax.bitwise_xor(zl // 2, t), 2)]


def spread_kernel(place, gathered, prev_row, next_row, *rest):
    outs, ten = rest[:4], rest[4]
    c, x = place[2], place[4]
    ten[0] = prev_row[...]
    ten[1:9] = gathered[...]
    ten[9] = next_row[...]
    for t, out in enumerate(outs):
        for i, core in enumerate((c, 1 - c)):
            out[i] = ten[pl.ds(2 * lax.rem(x + t, 4) + core, 3)]


def main_kernel(place, *refs):
    rows, (crossed, got, zw, xw), parts = refs[:4], refs[4:8], refs[8:12]
    out, keep, give, grid, force = refs[12:]
    y, c, x, odd_row = place[0], place[2], place[4], lax.rem(place[3], 2)
    for ref, i in ((keep, odd_row), (give, 1 - odd_row)):
        ref[...] = parts[0][i] + parts[1][i] + parts[2][i] + parts[3][i]

    for r in range(3):
        grid[r, :8] = jnp.zeros((8, WIDE), F32)
        grid[r, 200:] = jnp.zeros((8, WIDE), F32)
        for t in range(4):
            for h in range(2):
                mine, other = rows[t][0, r, h], crossed[t, r, h]
                first, second = jnp.where(c == 0, mine, other), jnp.where(c == 0, other, mine)
                at = pl.ds(pl.multiple_of(8 + 48 * lax.rem(x + 4 - t, 4) + 24 * h, 8), 24)
                grid[r, at, :LANES] = jnp.concatenate([first[:12], second[:12]], 0)
                grid[r, at, LANES:] = jnp.concatenate([first[12:], second[12:]], 0)
    here = grid[1, 8:200]
    low_lane = lax.broadcasted_iota(jnp.int32, (192, LANES), 1) < 64
    slopes = (
        (grid[1, 9:201] - grid[1, 7:199]) * 0.5,
        (grid[2, 8:200] - grid[0, 8:200]) * 0.5,
        (pltpu.roll(here, WIDE - 1, 1) - pltpu.roll(here, 1, 1)) * 0.5,
    )
    slopes = [(a[:, :LANES], jnp.where(low_lane, a[:, LANES:], pltpu.roll(a[:, LANES:], 64, 1))) for a in slopes]
    for k in range(8):
        at = slice(24 * k, 24 * k + 24)
        for b in range(6):
            r = jnp.concatenate([got[2 * k, 12 * b : 12 * b + 12], got[2 * k + 1, 12 * b : 12 * b + 12]], 0)
            for c in range(3):
                force[at, (c * 6 + b) * LANES : (c * 6 + b + 1) * LANES] = r * slopes[c][b // 4][at]

    def times(a1, a0, b1, b0):
        dot = lambda p, q: jnp.dot(p, q, preferred_element_type=F32)
        return dot(a1, b1) + (dot(a1, b0) + dot(a0, b1))

    smooth = times(zw[0], zw[1], *split(force[...]))

    for odd in range(2):
        left = []
        for s in (odd, odd + 2):
            for c in range(3):
                at = c * 6 * LANES
                left.append(
                    jnp.concatenate(
                        [
                            smooth[:, at + s * LANES : at + (s + 1) * LANES],
                            smooth[:, at + (4 + s // 2) * LANES : at + (5 + s // 2) * LANES],
                        ],
                        1,
                    )
                )
        update = times(*split(jnp.concatenate(left, 0)), xw[odd, 0], xw[odd, 1])
        for i, s in enumerate((odd, odd + 2)):
            to = 8 * lax.rem(y + 4 - s, 4)
            for c in range(3):
                for j in range(8):
                    at = (i * 3 + c) * 96 + 12 * j
                    piece = update[at : at + 12]
                    out[to + j, 12 * c : 12 * c + 12, :] = piece[:, :LANES]
                    out[to + j, 36 + 6 * c : 42 + 6 * c, :] = jnp.concatenate(
                        [piece[:6, LANES:], piece[6:, LANES:]], 1
                    )


def per_device(image, velocity, template, z_kernel, x_kernel):
    place = jnp.stack([lax.axis_index(a) for a in ("y", "zh", "c", "zl", "x")]).astype(jnp.int32)

    (piece,) = call(piece_kernel, (shape(16, 24, LANES),))(None, template)
    gathered = lax.all_to_all(piece, COL, 0, 0, tiled=True).reshape(8, 2, 24, LANES)

    *raws, zw, xw = call(
        pack_kernel,
        (
            *[shape(6, 12, 8, LANES)] * 4,
            jax.ShapeDtypeStruct((2, 96, 192), BF16),
            jax.ShapeDtypeStruct((2, 2, 256, 192), BF16),
        ),
    )(place, image[0], velocity[0], z_kernel, x_kernel)
    raws = [raws[0]] + [
        lax.ppermute(raws[s], "y", [(i, (i + s) % 4) for i in range(4)]) for s in (1, 2, 3)
    ]

    tmpl, ends, first, last = call(
        halo_kernel,
        (shape(2, 24, 8, LANES), shape(2, 4, 8, LANES), shape(2, 24, LANES), shape(2, 24, LANES)),
    )(place, gathered)
    by_core = lax.ppermute(ends, "c", [(0, 1), (1, 0)])
    by_x = lax.ppermute(ends, ("x", "c"), [(2 * i + 1, 2 * i + 2) for i in range(3)] + [(2 * i + 2, 2 * i + 1) for i in range(3)])
    prev_row = lax.ppermute(last, "y", [(i, i + 1) for i in range(3)])
    next_row = lax.ppermute(first, "y", [(i + 1, i) for i in range(3)])

    by_row, *parts = call(
        residual_kernel,
        (shape(16, 72, LANES), *[shape(2, 24, LANES)] * 4),
        (pltpu.VMEM((96, 8, LANES), F32), pltpu.VMEM((8, 24, LANES), F32)),
    )(place, tmpl, prev_row, next_row, by_core, by_x, *raws)
    got = lax.all_to_all(by_row, ("x", "zh", "c"), 0, 0, tiled=True)

    rows = list(
        call(spread_kernel, (shape(2, 3, 2, 24, LANES),) * 4, (pltpu.VMEM((10, 2, 24, LANES), F32),))(
            place, gathered, prev_row, next_row
        )
    )
    for t in (1, 2, 3):
        rows[t] = lax.ppermute(rows[t], "x", [(i, (i + t) % 4) for i in range(4)])
    crossed = lax.ppermute(jnp.stack([r[1] for r in rows]), "c", [(0, 1), (1, 0)])

    for t in (1, 2, 3):
        parts[t] = lax.ppermute(parts[t], "zl", [(i, i ^ (2 * t)) for i in range(8)])

    packed, keep, give = call(
        main_kernel,
        (shape(32, 54, LANES), shape(24, LANES), shape(24, LANES)),
        (pltpu.VMEM((3, 208, WIDE), F32), pltpu.VMEM((192, 18 * LANES), F32)),
    )(place, *rows, crossed, got, zw, xw, *parts)
    total = keep + lax.ppermute(give, "zl", [(i, i ^ 1) for i in range(8)])
    summed = jnp.concatenate([total[:12], total[12:, :64]], -1)[:, None]
    new_template = template + summed / 32

    back = lax.all_to_all(packed, ROW, 0, 0, tiled=True)
    low = back[:, :36].reshape(32, 3, 12, LANES)
    high = back[:, 36:].reshape(32, 3, 6, LANES)
    high = jnp.concatenate([high[..., :64], high[..., 64:]], 2)
    out = jnp.concatenate([low, high], -1).transpose(1, 2, 0, 3)
    return out[None], new_template


def solution(mesh):
    fine = Mesh(mesh.devices.reshape(4, 8, 4, 2, 2), ("y", "zl", "x", "zh", "c"))
    subj, slab = ("y", "zl"), ("x", "zh", "c")
    in_specs = (
        P(subj, slab, None, None),
        P(subj, None, slab, None, None),
        P(slab, subj, None),
        P(),
        P(),
    )
    out_specs = (P(subj, None, slab, None, None), P(slab, subj, None))
    return jax.shard_map(
        per_device, mesh=fine, in_specs=in_specs, out_specs=out_specs, check_vma=False
    )
```

```python
import jax
import jax.numpy as jnp
from jax import lax
from jax.experimental import pallas as pl
from jax.experimental.pallas import tpu as pltpu
from jax.sharding import Mesh, PartitionSpec as P

ROW = ("y", "x", "c")
COL = ("zl", "zh")
LANES, WIDE = 128, 256
F32 = jnp.float32
BF16 = jnp.bfloat16


def shape(*dims):
    return jax.ShapeDtypeStruct(dims, F32)


def held(*dims):
    return pltpu.VMEM(dims, F32)


def vmem(n):
    return [pl.BlockSpec(memory_space=pltpu.VMEM)] * n


def smem():
    return pl.BlockSpec(memory_space=pltpu.SMEM)


def call(kernel, outs, scratch=(), pin=True):
    def run(place, *args):
        if pin:
            args = [pltpu.with_memory_space_constraint(a, pltpu.VMEM) for a in args]
        first = [] if place is None else [place]
        return pl.pallas_call(
            kernel,
            out_shape=outs,
            in_specs=[*([smem()] * len(first)), *vmem(len(args))],
            out_specs=tuple(vmem(len(outs))),
            scratch_shapes=list(scratch),
        )(*first, *args)

    return run


def piece_kernel(row, out):
    values = row[:, 0, :]
    for i in range(16):
        out[i, :12, :] = values[:, :LANES]
        out[i, 12:, :] = jnp.concatenate([values[:, LANES:], jnp.zeros((12, 64), F32)], 1)


def split(a):
    top = a.astype(BF16)
    return top, (a - top.astype(F32)).astype(BF16)


def weights_kernel(place, zk, xk, zw, xw):
    zrows = [zk[pl.ds(pl.multiple_of(48 * x + 24 * place[1], 8), 24), :] for x in range(4)]
    zw[0], zw[1] = split(jnp.concatenate(zrows, 0))
    xt = xk[...].T
    zeros = jnp.zeros((64, 192), F32)
    for odd in range(2):
        cols = [xt[:LANES], zeros, xt[LANES:]] if odd else [xt[:LANES], xt[LANES:], zeros]
        xw[odd, 0], xw[odd, 1] = split(jnp.concatenate(cols, 0))


def pack_kernel(place, image, velocity, *outs):
    for s, out in enumerate(outs):
        at = pl.multiple_of(8 * lax.rem(place[0] + s, 4), 8)
        rows = pl.ds(at, 8)
        for a in range(4):
            src = image if a == 0 else velocity.at[a - 1]
            out[a] = src[:, rows, :LANES]
        for k in range(2):
            first = image if k == 0 else velocity.at[1]
            second = velocity.at[2 * k]
            out[4 + k] = jnp.concatenate([first[:, rows, LANES:], second[:, rows, LANES:]], -1)


def halo_kernel(place, gathered, tmpl, ends, first, last):
    for h in range(2):
        for k in range(3):
            block = jnp.swapaxes(gathered[:, h, 8 * k : 8 * k + 8], 0, 1)
            tmpl[h, 8 * k : 8 * k + 8] = block
            for i, p in enumerate((0, 11, 12, 23)):
                if p // 8 == k:
                    ends[h, i] = block[p % 8]
        first[h] = gathered[0, h]
        last[h] = gathered[7, h]


def residual_kernel(place, tmpl, prev_row, next_row, by_core, by_x, *rest):
    raws, out, parts, (rows, total) = rest[:4], rest[4], rest[5:9], rest[9:]
    zh, c, zl = place[1], place[2], place[3]
    low, high = tmpl[zh, :12], tmpl[zh, 12:]
    here = jnp.concatenate([low, high], -1)

    at_x = jnp.logical_and(c == 0, zh == 0)
    z_from = jnp.where(c == 0, 1 - zh, zh)
    before = jnp.where(
        at_x,
        jnp.concatenate([by_x[1, 1], by_x[1, 3]], -1),
        jnp.concatenate([by_core[z_from, 1], by_core[z_from, 3]], -1),
    )
    at_x = jnp.logical_and(c == 1, zh == 1)
    z_from = jnp.where(c == 0, zh, 1 - zh)
    after = jnp.where(
        at_x,
        jnp.concatenate([by_x[0, 0], by_x[0, 2]], -1),
        jnp.concatenate([by_core[z_from, 0], by_core[z_from, 2]], -1),
    )
    up = jnp.concatenate([here[1:], after[None]], 0)
    down = jnp.concatenate([before[None], here[:-1]], 0)
    slope_z = (up - down) * 0.5

    line = lax.broadcasted_iota(jnp.int32, (12, 8, WIDE), 1)

    def edge(ref):
        e = jnp.concatenate([ref[zh, :12], ref[zh, 12:]], -1)
        return jnp.broadcast_to(e[:, None, :], (12, 8, WIDE))

    up = jnp.where(line == 7, edge(next_row), pltpu.roll(here, 7, 1))
    down = jnp.where(line == 0, edge(prev_row), pltpu.roll(here, 1, 1))
    slope_y = (up - down) * 0.5
    slope_x = (pltpu.roll(here, WIDE - 1, 2) - pltpu.roll(here, 1, 2)) * 0.5

    slopes = (slope_z, slope_y, slope_x)
    lane = lax.broadcasted_iota(jnp.int32, (12, 8, LANES), 2)
    sum_low = jnp.zeros((12, 8, LANES), F32)
    sum_high = jnp.zeros((12, 8, LANES), F32)
    highs = []
    for s, raw in enumerate(raws):
        warped = here[..., :LANES]
        motion = raw[1] * slopes[0][..., :LANES] + raw[2] * slopes[1][..., :LANES] + raw[3] * slopes[2][..., :LANES]
        r_low = raw[0] - (warped + motion)
        zero_one, two_three = raw[4], raw[5]
        swap_01, swap_23 = pltpu.roll(zero_one, 64, 2), pltpu.roll(two_three, 64, 2)
        motion = swap_01 * slopes[0][..., LANES:] + two_three * slopes[1][..., LANES:] + swap_23 * slopes[2][..., LANES:]
        r_high = zero_one - (here[..., LANES:] + motion)
        rows[12 * s : 12 * s + 12] = r_low
        highs.append(r_high)
        sum_low += r_low
        sum_high += r_high
    for k in range(2):
        rows[48 + 12 * k : 60 + 12 * k] = jnp.where(lane < 64, highs[2 * k], pltpu.roll(highs[2 * k + 1], 64, 2))
    rows[72:84] = sum_low
    rows[84:] = sum_high
    for k in range(12):
        block = jnp.swapaxes(rows[8 * k : 8 * k + 8], 0, 1)
        if k >= 9:
            total[:, 8 * (k - 9) : 8 * (k - 8)] = block
            continue
        for i in range(8):
            x, core = i // 2, i % 2
            for h in range(2):
                out[4 * x + 2 * h + core, 8 * k : 8 * k + 8] = block[i]
    for t, part in enumerate(parts):
        part[...] = total[pl.ds(2 * lax.bitwise_xor(zl // 2, t), 2)]


def main_kernel(place, prev, mine, succ, got, zw, xw, *rest):
    parts, (out, keep, give, grid, force) = rest[:4], rest[4:]
    y, odd_row = place[0], lax.rem(place[3], 2)
    for ref, i in ((keep, odd_row), (give, 1 - odd_row)):
        ref[...] = parts[0][i] + parts[1][i] + parts[2][i] + parts[3][i]

    for r, ref in enumerate((prev, mine, succ)):
        grid[r, :8] = jnp.zeros((8, WIDE), F32)
        grid[r, 200:] = jnp.zeros((8, WIDE), F32)
        for x in range(4):
            for h in range(2):
                at = 8 + 48 * x + 24 * h
                first, second = ref[2 * x, h], ref[2 * x + 1, h]
                grid[r, at : at + 24, :LANES] = jnp.concatenate([first[:12], second[:12]], 0)
                grid[r, at : at + 24, LANES:] = jnp.concatenate([first[12:], second[12:]], 0)
    here = grid[1, 8:200]
    low_lane = lax.broadcasted_iota(jnp.int32, (192, LANES), 1) < 64
    slopes = (
        (grid[1, 9:201] - grid[1, 7:199]) * 0.5,
        (grid[2, 8:200] - grid[0, 8:200]) * 0.5,
        (pltpu.roll(here, WIDE - 1, 1) - pltpu.roll(here, 1, 1)) * 0.5,
    )
    slopes = [(a[:, :LANES], jnp.where(low_lane, a[:, LANES:], pltpu.roll(a[:, LANES:], 64, 1))) for a in slopes]
    for k in range(8):
        at = slice(24 * k, 24 * k + 24)
        for b in range(6):
            r = jnp.concatenate([got[2 * k, 12 * b : 12 * b + 12], got[2 * k + 1, 12 * b : 12 * b + 12]], 0)
            for c in range(3):
                force[at, (c * 6 + b) * LANES : (c * 6 + b + 1) * LANES] = r * slopes[c][b // 4][at]

    def times(a1, a0, b1, b0):
        dot = lambda p, q: jnp.dot(p, q, preferred_element_type=F32)
        return dot(a1, b1) + (dot(a1, b0) + dot(a0, b1))

    smooth = times(zw[0], zw[1], *split(force[...]))

    for odd in range(2):
        left = []
        for s in (odd, odd + 2):
            for c in range(3):
                at = c * 6 * LANES
                left.append(
                    jnp.concatenate(
                        [
                            smooth[:, at + s * LANES : at + (s + 1) * LANES],
                            smooth[:, at + (4 + s // 2) * LANES : at + (5 + s // 2) * LANES],
                        ],
                        1,
                    )
                )
        update = times(*split(jnp.concatenate(left, 0)), xw[odd, 0], xw[odd, 1])
        for i, s in enumerate((odd, odd + 2)):
            to = 8 * lax.rem(y + 4 - s, 4)
            for c in range(3):
                for j in range(8):
                    at = (i * 3 + c) * 96 + 12 * j
                    piece = update[at : at + 12]
                    out[to + j, 12 * c : 12 * c + 12, :] = piece[:, :LANES]
                    out[to + j, 36 + 6 * c : 42 + 6 * c, :] = jnp.concatenate(
                        [piece[:6, LANES:], piece[6:, LANES:]], 1
                    )


def per_device(image, velocity, template, z_kernel, x_kernel):
    place = jnp.stack([lax.axis_index(a) for a in ("y", "zh", "c", "zl")]).astype(jnp.int32)

    (piece,) = call(piece_kernel, (shape(16, 24, LANES),))(None, template)
    gathered = lax.all_to_all(piece, COL, 0, 0, tiled=True).reshape(8, 2, 24, LANES)

    raws = call(
        pack_kernel, (held(6, 12, 8, LANES), *[shape(6, 12, 8, LANES)] * 3), pin=False
    )(place, image[0], velocity[0])
    raws = [raws[0]] + [
        lax.ppermute(raws[s], "y", [(i, (i + s) % 4) for i in range(4)]) for s in (1, 2, 3)
    ]

    tmpl, ends, first, last = call(
        halo_kernel,
        (held(2, 24, 8, LANES), *[shape(2, 4, 8, LANES), shape(2, 24, LANES), shape(2, 24, LANES)]),
    )(place, gathered)
    by_core = lax.ppermute(ends, "c", [(0, 1), (1, 0)])
    by_x = lax.ppermute(ends, ("x", "c"), [(2 * i + 1, 2 * i + 2) for i in range(3)] + [(2 * i + 2, 2 * i + 1) for i in range(3)])
    prev_row = lax.ppermute(last, "y", [(i, i + 1) for i in range(3)])
    next_row = lax.ppermute(first, "y", [(i + 1, i) for i in range(3)])

    gathered, by_x = lax.optimization_barrier((gathered, by_x))
    mine = lax.all_to_all(gathered, ("x", "c"), 0, 0, tiled=True)

    by_row, *parts = call(
        residual_kernel,
        (shape(16, 72, LANES), held(2, 24, LANES), *[shape(2, 24, LANES)] * 3),
        (pltpu.VMEM((96, 8, LANES), F32), pltpu.VMEM((8, 24, LANES), F32)),
    )(place, tmpl, prev_row, next_row, by_core, by_x, *raws)
    by_row, mine = lax.optimization_barrier((by_row, mine))
    got = lax.all_to_all(by_row, ("x", "zh", "c"), 0, 0, tiled=True)

    along = [(i, i + 1) for i in range(31)]
    prev = lax.ppermute(mine, ROW, along)
    succ = lax.ppermute(mine, ROW, [(j, i) for i, j in along])
    zw, xw = call(
        weights_kernel,
        (pltpu.VMEM((2, 96, 192), BF16), pltpu.VMEM((2, 2, 256, 192), BF16)),
    )(place, z_kernel, x_kernel)

    for t in (1, 2, 3):
        parts[t] = lax.ppermute(parts[t], "zl", [(i, i ^ (2 * t)) for i in range(8)])

    packed, keep, give = call(
        main_kernel,
        (shape(32, 54, LANES), shape(24, LANES), shape(24, LANES)),
        (pltpu.VMEM((3, 208, WIDE), F32), pltpu.VMEM((192, 18 * LANES), F32)),
    )(place, prev, mine, succ, got, zw, xw, *parts)
    total = keep + lax.ppermute(give, "zl", [(i, i ^ 1) for i in range(8)])
    summed = jnp.concatenate([total[:12], total[12:, :64]], -1)[:, None]
    new_template = template + summed / 32

    back = lax.all_to_all(packed, ROW, 0, 0, tiled=True)
    low = back[:, :36].reshape(32, 3, 12, LANES)
    high = back[:, 36:].reshape(32, 3, 6, LANES)
    high = jnp.concatenate([high[..., :64], high[..., 64:]], 2)
    out = jnp.concatenate([low, high], -1).transpose(1, 2, 0, 3)
    return out[None], new_template


def solution(mesh):
    fine = Mesh(mesh.devices.reshape(4, 8, 4, 2, 2), ("y", "zl", "x", "zh", "c"))
    subj, slab = ("y", "zl"), ("x", "zh", "c")
    in_specs = (
        P(subj, slab, None, None),
        P(subj, None, slab, None, None),
        P(slab, subj, None),
        P(),
        P(),
    )
    out_specs = (P(subj, None, slab, None, None), P(slab, subj, None))
    return jax.shard_map(
        per_device, mesh=fine, in_specs=in_specs, out_specs=out_specs, check_vma=False
    )
```

```python
import jax
import jax.numpy as jnp
from jax import lax
from jax.experimental import pallas as pl
from jax.experimental.pallas import tpu as pltpu
from jax.sharding import Mesh, PartitionSpec as P

ROW = ("y", "x", "c")
COL = ("zl", "zh")
LANES, WIDE = 128, 256
F32 = jnp.float32
BF16 = jnp.bfloat16


def shape(*dims):
    return jax.ShapeDtypeStruct(dims, F32)


def held(*dims):
    return pltpu.VMEM(dims, F32)


def vmem(n):
    return [pl.BlockSpec(memory_space=pltpu.VMEM)] * n


def smem():
    return pl.BlockSpec(memory_space=pltpu.SMEM)


def call(kernel, outs, scratch=(), pin=True):
    def run(place, *args):
        if pin:
            args = [pltpu.with_memory_space_constraint(a, pltpu.VMEM) for a in args]
        first = [] if place is None else [place]
        return pl.pallas_call(
            kernel,
            out_shape=outs,
            in_specs=[*([smem()] * len(first)), *vmem(len(args))],
            out_specs=tuple(vmem(len(outs))),
            scratch_shapes=list(scratch),
        )(*first, *args)

    return run


def piece_kernel(row, out):
    values = row[:, 0, :]
    for i in range(16):
        out[i, :12, :] = values[:, :LANES]
        out[i, 12:, :] = jnp.concatenate([values[:, LANES:], jnp.zeros((12, 64), F32)], 1)


def split(a):
    top = a.astype(BF16)
    return top, (a - top.astype(F32)).astype(BF16)


def weights_kernel(place, zk, xk, zw, xw):
    zrows = [zk[pl.ds(pl.multiple_of(48 * x + 24 * place[1], 8), 24), :] for x in range(4)]
    zw[0], zw[1] = split(jnp.concatenate(zrows, 0))
    xt = xk[...].T
    zeros = jnp.zeros((64, 192), F32)
    for odd in range(2):
        cols = [xt[:LANES], zeros, xt[LANES:]] if odd else [xt[:LANES], xt[LANES:], zeros]
        xw[odd, 0], xw[odd, 1] = split(jnp.concatenate(cols, 0))


def pack_kernel(place, image, velocity, *outs):
    for s, out in enumerate(outs):
        at = pl.multiple_of(8 * lax.rem(place[0] + s, 4), 8)
        rows = pl.ds(at, 8)
        for a in range(4):
            src = image if a == 0 else velocity.at[a - 1]
            out[a] = src[:, rows, :LANES]
        for k in range(2):
            first = image if k == 0 else velocity.at[1]
            second = velocity.at[2 * k]
            out[4 + k] = jnp.concatenate([first[:, rows, LANES:], second[:, rows, LANES:]], -1)


def halo_kernel(place, gathered, tmpl, ends, first, last):
    for h in range(2):
        for k in range(3):
            block = jnp.swapaxes(gathered[:, h, 8 * k : 8 * k + 8], 0, 1)
            tmpl[h, 8 * k : 8 * k + 8] = block
            for i, p in enumerate((0, 11, 12, 23)):
                if p // 8 == k:
                    ends[h, i] = block[p % 8]
        first[h] = gathered[0, h]
        last[h] = gathered[7, h]


def residual_kernel(place, tmpl, prev_row, next_row, by_core, by_x, *rest):
    raws, out, parts, (rows, total) = rest[:4], rest[4], rest[5:9], rest[9:]
    zh, c, zl = place[1], place[2], place[3]
    low, high = tmpl[zh, :12], tmpl[zh, 12:]
    here = jnp.concatenate([low, high], -1)

    at_x = jnp.logical_and(c == 0, zh == 0)
    z_from = jnp.where(c == 0, 1 - zh, zh)
    before = jnp.where(
        at_x,
        jnp.concatenate([by_x[1, 1], by_x[1, 3]], -1),
        jnp.concatenate([by_core[z_from, 1], by_core[z_from, 3]], -1),
    )
    at_x = jnp.logical_and(c == 1, zh == 1)
    z_from = jnp.where(c == 0, zh, 1 - zh)
    after = jnp.where(
        at_x,
        jnp.concatenate([by_x[0, 0], by_x[0, 2]], -1),
        jnp.concatenate([by_core[z_from, 0], by_core[z_from, 2]], -1),
    )
    up = jnp.concatenate([here[1:], after[None]], 0)
    down = jnp.concatenate([before[None], here[:-1]], 0)
    slope_z = (up - down) * 0.5

    line = lax.broadcasted_iota(jnp.int32, (12, 8, WIDE), 1)

    def edge(ref):
        e = jnp.concatenate([ref[zh, :12], ref[zh, 12:]], -1)
        return jnp.broadcast_to(e[:, None, :], (12, 8, WIDE))

    up = jnp.where(line == 7, edge(next_row), pltpu.roll(here, 7, 1))
    down = jnp.where(line == 0, edge(prev_row), pltpu.roll(here, 1, 1))
    slope_y = (up - down) * 0.5
    slope_x = (pltpu.roll(here, WIDE - 1, 2) - pltpu.roll(here, 1, 2)) * 0.5

    slopes = (slope_z, slope_y, slope_x)
    lane = lax.broadcasted_iota(jnp.int32, (12, 8, LANES), 2)
    sum_low = jnp.zeros((12, 8, LANES), F32)
    sum_high = jnp.zeros((12, 8, LANES), F32)
    highs = []
    for s, raw in enumerate(raws):
        warped = here[..., :LANES]
        motion = raw[1] * slopes[0][..., :LANES] + raw[2] * slopes[1][..., :LANES] + raw[3] * slopes[2][..., :LANES]
        r_low = raw[0] - (warped + motion)
        zero_one, two_three = raw[4], raw[5]
        swap_01, swap_23 = pltpu.roll(zero_one, 64, 2), pltpu.roll(two_three, 64, 2)
        motion = swap_01 * slopes[0][..., LANES:] + two_three * slopes[1][..., LANES:] + swap_23 * slopes[2][..., LANES:]
        r_high = zero_one - (here[..., LANES:] + motion)
        rows[12 * s : 12 * s + 12] = r_low
        highs.append(r_high)
        sum_low += r_low
        sum_high += r_high
    for k in range(2):
        rows[48 + 12 * k : 60 + 12 * k] = jnp.where(lane < 64, highs[2 * k], pltpu.roll(highs[2 * k + 1], 64, 2))
    rows[72:84] = sum_low
    rows[84:] = sum_high
    for k in range(12):
        block = jnp.swapaxes(rows[8 * k : 8 * k + 8], 0, 1)
        if k >= 9:
            total[:, 8 * (k - 9) : 8 * (k - 8)] = block
            continue
        for i in range(8):
            x, core = i // 2, i % 2
            for h in range(2):
                out[4 * x + 2 * h + core, 8 * k : 8 * k + 8] = block[i]
    for t, part in enumerate(parts):
        part[...] = total[pl.ds(2 * lax.bitwise_xor(zl // 2, t), 2)]


def main_kernel(place, prev, mine, succ, got, zw, xw, *rest):
    out, grid, force = rest
    y = place[0]

    for r, ref in enumerate((prev, mine, succ)):
        grid[r, :8] = jnp.zeros((8, WIDE), F32)
        grid[r, 200:] = jnp.zeros((8, WIDE), F32)
        for x in range(4):
            for h in range(2):
                at = 8 + 48 * x + 24 * h
                first, second = ref[2 * x, h], ref[2 * x + 1, h]
                grid[r, at : at + 24, :LANES] = jnp.concatenate([first[:12], second[:12]], 0)
                grid[r, at : at + 24, LANES:] = jnp.concatenate([first[12:], second[12:]], 0)
    here = grid[1, 8:200]
    low_lane = lax.broadcasted_iota(jnp.int32, (192, LANES), 1) < 64
    slopes = (
        (grid[1, 9:201] - grid[1, 7:199]) * 0.5,
        (grid[2, 8:200] - grid[0, 8:200]) * 0.5,
        (pltpu.roll(here, WIDE - 1, 1) - pltpu.roll(here, 1, 1)) * 0.5,
    )
    slopes = [(a[:, :LANES], jnp.where(low_lane, a[:, LANES:], pltpu.roll(a[:, LANES:], 64, 1))) for a in slopes]
    for k in range(8):
        at = slice(24 * k, 24 * k + 24)
        for b in range(6):
            r = jnp.concatenate([got[2 * k, 12 * b : 12 * b + 12], got[2 * k + 1, 12 * b : 12 * b + 12]], 0)
            for c in range(3):
                force[at, (c * 6 + b) * LANES : (c * 6 + b + 1) * LANES] = r * slopes[c][b // 4][at]

    def times(a1, a0, b1, b0):
        dot = lambda p, q: jnp.dot(p, q, preferred_element_type=F32)
        return dot(a1, b1) + (dot(a1, b0) + dot(a0, b1))

    smooth = times(zw[0], zw[1], *split(force[...]))

    for odd in range(2):
        left = []
        for s in (odd, odd + 2):
            for c in range(3):
                at = c * 6 * LANES
                left.append(
                    jnp.concatenate(
                        [
                            smooth[:, at + s * LANES : at + (s + 1) * LANES],
                            smooth[:, at + (4 + s // 2) * LANES : at + (5 + s // 2) * LANES],
                        ],
                        1,
                    )
                )
        update = times(*split(jnp.concatenate(left, 0)), xw[odd, 0], xw[odd, 1])
        for i, s in enumerate((odd, odd + 2)):
            to = 8 * lax.rem(y + 4 - s, 4)
            for c in range(3):
                for j in range(8):
                    at = (i * 3 + c) * 96 + 12 * j
                    piece = update[at : at + 12]
                    out[to + j, 12 * c : 12 * c + 12, :] = piece[:, :LANES]
                    out[to + j, 36 + 6 * c : 42 + 6 * c, :] = jnp.concatenate(
                        [piece[:6, LANES:], piece[6:, LANES:]], 1
                    )


def unpack_kernel(packed, out):
    for k in range(4):
        rows = slice(8 * k, 8 * k + 8)
        block = jnp.swapaxes(packed[rows], 0, 1)
        for c in range(3):
            out[c, :, rows, :LANES] = block[12 * c : 12 * c + 12]
            high = block[36 + 6 * c : 42 + 6 * c]
            out[c, :6, rows, LANES:] = high[..., :64]
            out[c, 6:, rows, LANES:] = high[..., 64:]


def per_device(image, velocity, template, z_kernel, x_kernel):
    place = jnp.stack([lax.axis_index(a) for a in ("y", "zh", "c", "zl")]).astype(jnp.int32)

    (piece,) = call(piece_kernel, (shape(16, 24, LANES),))(None, template)
    gathered = lax.all_to_all(piece, COL, 0, 0, tiled=True).reshape(8, 2, 24, LANES)

    raws = call(
        pack_kernel, (held(6, 12, 8, LANES), *[shape(6, 12, 8, LANES)] * 3), pin=False
    )(place, image[0], velocity[0])
    raws = [raws[0]] + [
        lax.ppermute(raws[s], "y", [(i, (i + s) % 4) for i in range(4)]) for s in (1, 2, 3)
    ]

    tmpl, ends, first, last = call(
        halo_kernel,
        (held(2, 24, 8, LANES), *[shape(2, 4, 8, LANES), shape(2, 24, LANES), shape(2, 24, LANES)]),
    )(place, gathered)
    by_core = lax.ppermute(ends, "c", [(0, 1), (1, 0)])
    by_x = lax.ppermute(ends, ("x", "c"), [(2 * i + 1, 2 * i + 2) for i in range(3)] + [(2 * i + 2, 2 * i + 1) for i in range(3)])
    prev_row = lax.ppermute(last, "y", [(i, i + 1) for i in range(3)])
    next_row = lax.ppermute(first, "y", [(i + 1, i) for i in range(3)])

    mine = lax.all_to_all(gathered, ("x", "c"), 0, 0, tiled=True)

    by_row, *parts = call(
        residual_kernel,
        (shape(16, 72, LANES), held(2, 24, LANES), *[shape(2, 24, LANES)] * 3),
        (pltpu.VMEM((96, 8, LANES), F32), pltpu.VMEM((8, 24, LANES), F32)),
    )(place, tmpl, prev_row, next_row, by_core, by_x, *raws)
    by_row, mine = lax.optimization_barrier((by_row, mine))
    got = lax.all_to_all(by_row, ("x", "zh", "c"), 0, 0, tiled=True)

    along = [(i, i + 1) for i in range(31)]
    prev = lax.ppermute(mine, ROW, along)
    succ = lax.ppermute(mine, ROW, [(j, i) for i, j in along])
    zw, xw = call(
        weights_kernel,
        (pltpu.VMEM((2, 96, 192), BF16), pltpu.VMEM((2, 2, 256, 192), BF16)),
    )(place, z_kernel, x_kernel)

    packed, = call(
        main_kernel,
        (shape(32, 54, LANES),),
        (pltpu.VMEM((3, 208, WIDE), F32), pltpu.VMEM((192, 18 * LANES), F32)),
    )(place, prev, mine, succ, got, zw, xw)
    for t in (1, 2, 3):
        parts[t] = lax.ppermute(parts[t], "zl", [(i, i ^ (2 * t)) for i in range(8)])
    two, odd = sum(parts), lax.axis_index("zl") & 1
    keep = lax.dynamic_index_in_dim(two, odd, 0, False)
    give = lax.dynamic_index_in_dim(two, 1 - odd, 0, False)
    total = keep + lax.ppermute(give, "zl", [(i, i ^ 1) for i in range(8)])
    summed = jnp.concatenate([total[:12], total[12:, :64]], -1)[:, None]
    new_template = template + summed / 32

    back = lax.all_to_all(packed, ROW, 0, 0, tiled=True)
    (out,) = call(unpack_kernel, (shape(3, 12, 32, 192),))(None, back)
    return out[None], new_template


def solution(mesh):
    fine = Mesh(mesh.devices.reshape(4, 8, 4, 2, 2), ("y", "zl", "x", "zh", "c"))
    subj, slab = ("y", "zl"), ("x", "zh", "c")
    in_specs = (
        P(subj, slab, None, None),
        P(subj, None, slab, None, None),
        P(slab, subj, None),
        P(),
        P(),
    )
    out_specs = (P(subj, None, slab, None, None), P(slab, subj, None))
    return jax.shard_map(
        per_device, mesh=fine, in_specs=in_specs, out_specs=out_specs, check_vma=False
    )
```

```python
import jax
import jax.numpy as jnp
from jax import lax
from jax.experimental import pallas as pl
from jax.experimental.pallas import tpu as pltpu
from jax.sharding import Mesh, PartitionSpec as P

ROW = ("y", "x", "c")
COL = ("zl", "zh")
LANES, WIDE = 128, 256
F32 = jnp.float32
BF16 = jnp.bfloat16


def shape(*dims):
    return jax.ShapeDtypeStruct(dims, F32)


def held(*dims):
    return pltpu.VMEM(dims, F32)


def vmem(n):
    return [pl.BlockSpec(memory_space=pltpu.VMEM)] * n


def smem():
    return pl.BlockSpec(memory_space=pltpu.SMEM)


def call(kernel, outs, scratch=(), pin=True):
    def run(place, *args):
        if pin:
            args = [pltpu.with_memory_space_constraint(a, pltpu.VMEM) for a in args]
        first = [] if place is None else [place]
        return pl.pallas_call(
            kernel,
            out_shape=outs,
            in_specs=[*([smem()] * len(first)), *vmem(len(args))],
            out_specs=tuple(vmem(len(outs))),
            scratch_shapes=list(scratch),
        )(*first, *args)

    return run


def piece_kernel(row, out):
    values = row[:, 0, :]
    for i in range(16):
        out[i, :12, :] = values[:, :LANES]
        out[i, 12:, :] = jnp.concatenate([values[:, LANES:], jnp.zeros((12, 64), F32)], 1)


def split(a):
    top = a.astype(BF16)
    return top, (a - top.astype(F32)).astype(BF16)


def weights_kernel(place, zk, xk, zw, xw):
    zrows = [zk[pl.ds(pl.multiple_of(48 * x + 24 * place[1], 8), 24), :] for x in range(4)]
    zw[0], zw[1] = split(jnp.concatenate(zrows, 0))
    xt = xk[...].T
    zeros = jnp.zeros((64, 192), F32)
    for odd in range(2):
        cols = [xt[:LANES], zeros, xt[LANES:]] if odd else [xt[:LANES], xt[LANES:], zeros]
        xw[odd, 0], xw[odd, 1] = split(jnp.concatenate(cols, 0))


def pack_kernel(place, image, velocity, *outs):
    for s, out in enumerate(outs):
        at = pl.multiple_of(8 * lax.rem(place[0] + s, 4), 8)
        rows = pl.ds(at, 8)
        for a in range(4):
            src = image if a == 0 else velocity.at[a - 1]
            out[a] = src[:, rows, :LANES]
        for k in range(2):
            first = image if k == 0 else velocity.at[1]
            second = velocity.at[2 * k]
            out[4 + k] = jnp.concatenate([first[:, rows, LANES:], second[:, rows, LANES:]], -1)


def spread_kernel(place, gathered, tmpl, out):
    zh, c = place[1], place[2]
    for h in range(2):
        for k in range(3):
            tmpl[h, 8 * k : 8 * k + 8] = jnp.swapaxes(gathered[:, h, 8 * k : 8 * k + 8], 0, 1)
    near, far = 11 * (1 - c), 11 * c
    ends = [tmpl[zh, near], tmpl[zh, 12 + near], tmpl[1 - zh, far], tmpl[1 - zh, 12 + far]]
    for i in range(8):
        out[i, :24] = gathered[i, 0]
        out[i, 24:48] = gathered[i, 1]
        for k, end in enumerate(ends):
            out[i, 48 + 8 * k : 56 + 8 * k] = end


def residual_kernel(place, tmpl, prev_row, next_row, mixed, *rest):
    raws, out, parts, (rows, total) = rest[:4], rest[4], rest[5:9], rest[9:]
    zh, c, zl, x = place[1], place[2], place[3], place[4]
    low, high = tmpl[zh, :12], tmpl[zh, 12:]
    here = jnp.concatenate([low, high], -1)

    step = jnp.where(c == 0, zh - 1, zh)
    inside = jnp.logical_and(x + step >= 0, x + step < 4)
    chip = jnp.clip(x + step, 0, 3)
    near = jnp.concatenate([mixed[2 * x + 1 - c, 48:56], mixed[2 * x + 1 - c, 56:64]], -1)
    far = jnp.concatenate([mixed[2 * chip + 1 - c, 64:72], mixed[2 * chip + 1 - c, 72:80]], -1)
    far = jnp.where(inside, far, 0.0)
    before, after = jnp.where(c == 0, far, near), jnp.where(c == 0, near, far)
    up = jnp.concatenate([here[1:], after[None]], 0)
    down = jnp.concatenate([before[None], here[:-1]], 0)
    slope_z = (up - down) * 0.5

    line = lax.broadcasted_iota(jnp.int32, (12, 8, WIDE), 1)

    def edge(ref):
        e = jnp.concatenate([ref[zh, :12], ref[zh, 12:]], -1)
        return jnp.broadcast_to(e[:, None, :], (12, 8, WIDE))

    up = jnp.where(line == 7, edge(next_row), pltpu.roll(here, 7, 1))
    down = jnp.where(line == 0, edge(prev_row), pltpu.roll(here, 1, 1))
    slope_y = (up - down) * 0.5
    slope_x = (pltpu.roll(here, WIDE - 1, 2) - pltpu.roll(here, 1, 2)) * 0.5

    slopes = (slope_z, slope_y, slope_x)
    lane = lax.broadcasted_iota(jnp.int32, (12, 8, LANES), 2)
    sum_low = jnp.zeros((12, 8, LANES), F32)
    sum_high = jnp.zeros((12, 8, LANES), F32)
    highs = []
    for s, raw in enumerate(raws):
        warped = here[..., :LANES]
        motion = raw[1] * slopes[0][..., :LANES] + raw[2] * slopes[1][..., :LANES] + raw[3] * slopes[2][..., :LANES]
        r_low = raw[0] - (warped + motion)
        zero_one, two_three = raw[4], raw[5]
        swap_01, swap_23 = pltpu.roll(zero_one, 64, 2), pltpu.roll(two_three, 64, 2)
        motion = swap_01 * slopes[0][..., LANES:] + two_three * slopes[1][..., LANES:] + swap_23 * slopes[2][..., LANES:]
        r_high = zero_one - (here[..., LANES:] + motion)
        rows[12 * s : 12 * s + 12] = r_low
        highs.append(r_high)
        sum_low += r_low
        sum_high += r_high
    for k in range(2):
        rows[48 + 12 * k : 60 + 12 * k] = jnp.where(lane < 64, highs[2 * k], pltpu.roll(highs[2 * k + 1], 64, 2))
    rows[72:84] = sum_low
    rows[84:] = sum_high
    for k in range(12):
        block = jnp.swapaxes(rows[8 * k : 8 * k + 8], 0, 1)
        if k >= 9:
            total[:, 8 * (k - 9) : 8 * (k - 8)] = block
            continue
        for i in range(8):
            x, core = i // 2, i % 2
            for h in range(2):
                out[4 * x + 2 * h + core, 8 * k : 8 * k + 8] = block[i]
    for t, part in enumerate(parts):
        part[...] = total[pl.ds(2 * lax.bitwise_xor(zl // 2, t), 2)]


def main_kernel(place, prev, mine, succ, got, zw, xw, *rest):
    out, grid, force = rest
    y = place[0]

    for r, ref in enumerate((prev, mine, succ)):
        grid[r, :8] = jnp.zeros((8, WIDE), F32)
        grid[r, 200:] = jnp.zeros((8, WIDE), F32)
        for x in range(4):
            for h in range(2):
                at = 8 + 48 * x + 24 * h
                first, second = (ref[2 * x + c, 24 * h : 24 * h + 24] for c in range(2))
                grid[r, at : at + 24, :LANES] = jnp.concatenate([first[:12], second[:12]], 0)
                grid[r, at : at + 24, LANES:] = jnp.concatenate([first[12:], second[12:]], 0)
    here = grid[1, 8:200]
    low_lane = lax.broadcasted_iota(jnp.int32, (192, LANES), 1) < 64
    slopes = (
        (grid[1, 9:201] - grid[1, 7:199]) * 0.5,
        (grid[2, 8:200] - grid[0, 8:200]) * 0.5,
        (pltpu.roll(here, WIDE - 1, 1) - pltpu.roll(here, 1, 1)) * 0.5,
    )
    slopes = [(a[:, :LANES], jnp.where(low_lane, a[:, LANES:], pltpu.roll(a[:, LANES:], 64, 1))) for a in slopes]
    for k in range(8):
        at = slice(24 * k, 24 * k + 24)
        for b in range(6):
            r = jnp.concatenate([got[2 * k, 12 * b : 12 * b + 12], got[2 * k + 1, 12 * b : 12 * b + 12]], 0)
            for c in range(3):
                force[at, (c * 6 + b) * LANES : (c * 6 + b + 1) * LANES] = r * slopes[c][b // 4][at]

    def times(a1, a0, b1, b0):
        dot = lambda p, q: jnp.dot(p, q, preferred_element_type=F32)
        return dot(a1, b1) + (dot(a1, b0) + dot(a0, b1))

    smooth = times(zw[0], zw[1], *split(force[...]))

    for odd in range(2):
        left = []
        for s in (odd, odd + 2):
            for c in range(3):
                at = c * 6 * LANES
                left.append(
                    jnp.concatenate(
                        [
                            smooth[:, at + s * LANES : at + (s + 1) * LANES],
                            smooth[:, at + (4 + s // 2) * LANES : at + (5 + s // 2) * LANES],
                        ],
                        1,
                    )
                )
        update = times(*split(jnp.concatenate(left, 0)), xw[odd, 0], xw[odd, 1])
        for i, s in enumerate((odd, odd + 2)):
            to = 8 * lax.rem(y + 4 - s, 4)
            for c in range(3):
                for j in range(8):
                    at = (i * 3 + c) * 96 + 12 * j
                    piece = update[at : at + 12]
                    out[to + j, 12 * c : 12 * c + 12, :] = piece[:, :LANES]
                    out[to + j, 36 + 6 * c : 42 + 6 * c, :] = jnp.concatenate(
                        [piece[:6, LANES:], piece[6:, LANES:]], 1
                    )


def unpack_kernel(packed, out):
    for k in range(4):
        rows = slice(8 * k, 8 * k + 8)
        block = jnp.swapaxes(packed[rows], 0, 1)
        for c in range(3):
            out[c, :, rows, :LANES] = block[12 * c : 12 * c + 12]
            high = block[36 + 6 * c : 42 + 6 * c]
            out[c, :6, rows, LANES:] = high[..., :64]
            out[c, 6:, rows, LANES:] = high[..., 64:]


def per_device(image, velocity, template, z_kernel, x_kernel):
    place = jnp.stack([lax.axis_index(a) for a in ("y", "zh", "c", "zl", "x")]).astype(jnp.int32)

    (piece,) = call(piece_kernel, (shape(16, 24, LANES),))(None, template)
    gathered = lax.all_to_all(piece, COL, 0, 0, tiled=True).reshape(8, 2, 24, LANES)

    raws = call(
        pack_kernel, (held(6, 12, 8, LANES), *[shape(6, 12, 8, LANES)] * 3), pin=False
    )(place, image[0], velocity[0])
    raws = list(raws)
    for s in (2, 1, 3):
        raws[s] = lax.ppermute(raws[s], "y", [(i, (i + s) % 4) for i in range(4)])

    prev_row = lax.ppermute(gathered[7], "y", [(i, i + 1) for i in range(3)])
    next_row = lax.ppermute(gathered[0], "y", [(i + 1, i) for i in range(3)])
    tmpl, mixed = call(spread_kernel, (held(2, 24, 8, LANES), shape(8, 80, LANES)))(place, gathered)
    mixed = lax.all_to_all(mixed, ("x", "c"), 0, 0, tiled=True)

    by_row, *parts = call(
        residual_kernel,
        (shape(16, 72, LANES), held(2, 24, LANES), *[shape(2, 24, LANES)] * 3),
        (pltpu.VMEM((96, 8, LANES), F32), pltpu.VMEM((8, 24, LANES), F32)),
    )(place, tmpl, prev_row, next_row, mixed, *raws)
    got = lax.all_to_all(by_row, ("x", "zh", "c"), 0, 0, tiled=True)

    along = [(i, i + 1) for i in range(31)]
    prev = lax.ppermute(mixed, ROW, along)
    succ = lax.ppermute(mixed, ROW, [(j, i) for i, j in along])
    zw, xw = call(
        weights_kernel,
        (pltpu.VMEM((2, 96, 192), BF16), pltpu.VMEM((2, 2, 256, 192), BF16)),
    )(place, z_kernel, x_kernel)

    packed, = call(
        main_kernel,
        (shape(32, 54, LANES),),
        (pltpu.VMEM((3, 208, WIDE), F32), pltpu.VMEM((192, 18 * LANES), F32)),
    )(place, prev, mixed, succ, got, zw, xw)
    for t in (1, 2, 3):
        parts[t] = lax.ppermute(parts[t], "zl", [(i, i ^ (2 * t)) for i in range(8)])
    two, odd = sum(parts), lax.axis_index("zl") & 1
    keep = lax.dynamic_index_in_dim(two, odd, 0, False)
    give = lax.dynamic_index_in_dim(two, 1 - odd, 0, False)
    total = keep + lax.ppermute(give, "zl", [(i, i ^ 1) for i in range(8)])
    summed = jnp.concatenate([total[:12], total[12:, :64]], -1)[:, None]
    new_template = template + summed / 32

    back = lax.all_to_all(packed, ROW, 0, 0, tiled=True)
    (out,) = call(unpack_kernel, (shape(3, 12, 32, 192),))(None, back)
    return out[None], new_template


def solution(mesh):
    fine = Mesh(mesh.devices.reshape(4, 8, 4, 2, 2), ("y", "zl", "x", "zh", "c"))
    subj, slab = ("y", "zl"), ("x", "zh", "c")
    in_specs = (
        P(subj, slab, None, None),
        P(subj, None, slab, None, None),
        P(slab, subj, None),
        P(),
        P(),
    )
    out_specs = (P(subj, None, slab, None, None), P(slab, subj, None))
    return jax.shard_map(
        per_device, mesh=fine, in_specs=in_specs, out_specs=out_specs, check_vma=False
    )
```

```python
import jax
import jax.numpy as jnp
from jax import lax
from jax.experimental import pallas as pl
from jax.experimental.pallas import tpu as pltpu
from jax.sharding import Mesh, PartitionSpec as P

ROW = ("y", "x", "c")
COL = ("zl", "zh")
LANES, WIDE = 128, 256
F32 = jnp.float32
BF16 = jnp.bfloat16


def shape(*dims):
    return jax.ShapeDtypeStruct(dims, F32)


def held(*dims):
    return pltpu.VMEM(dims, F32)


def vmem(n):
    return [pl.BlockSpec(memory_space=pltpu.VMEM)] * n


def smem():
    return pl.BlockSpec(memory_space=pltpu.SMEM)


def call(kernel, outs, scratch=(), pin=True):
    def run(place, *args):
        if pin:
            args = [pltpu.with_memory_space_constraint(a, pltpu.VMEM) for a in args]
        first = [] if place is None else [place]
        return pl.pallas_call(
            kernel,
            out_shape=outs,
            in_specs=[*([smem()] * len(first)), *vmem(len(args))],
            out_specs=tuple(vmem(len(outs))),
            scratch_shapes=list(scratch),
        )(*first, *args)

    return run


def piece_kernel(row, out):
    values = row[:, 0, :]
    for i in range(16):
        out[i, :12, :] = values[:, :LANES]
        out[i, 12:, :] = jnp.concatenate([values[:, LANES:], jnp.zeros((12, 64), F32)], 1)


def split(a):
    top = a.astype(BF16)
    return top, (a - top.astype(F32)).astype(BF16)


def weights_kernel(place, zk, xk, zw, xw):
    zrows = [zk[pl.ds(pl.multiple_of(48 * x + 24 * place[1], 8), 24), :] for x in range(4)]
    zw[0], zw[1] = split(jnp.concatenate(zrows, 0))
    xt = xk[...].T
    zeros = jnp.zeros((64, 192), F32)
    for odd in range(2):
        cols = [xt[:LANES], zeros, xt[LANES:]] if odd else [xt[:LANES], xt[LANES:], zeros]
        xw[odd, 0], xw[odd, 1] = split(jnp.concatenate(cols, 0))


def pack_kernel(place, image, velocity, *outs):
    for s, out in enumerate(outs):
        at = pl.multiple_of(8 * lax.rem(place[0] + s, 4), 8)
        rows = pl.ds(at, 8)
        for a in range(4):
            src = image if a == 0 else velocity.at[a - 1]
            out[a] = src[:, rows, :LANES]
        for k in range(2):
            first = image if k == 0 else velocity.at[1]
            second = velocity.at[2 * k]
            out[4 + k] = jnp.concatenate([first[:, rows, LANES:], second[:, rows, LANES:]], -1)


def spread_kernel(place, gathered, tmpl, out):
    zh, c = place[1], place[2]
    for h in range(2):
        for k in range(3):
            tmpl[h, 8 * k : 8 * k + 8] = jnp.swapaxes(gathered[:, h, 8 * k : 8 * k + 8], 0, 1)
    near, far = 11 * (1 - c), 11 * c
    ends = [tmpl[zh, near], tmpl[zh, 12 + near], tmpl[1 - zh, far], tmpl[1 - zh, 12 + far]]
    for i in range(8):
        out[i, :24] = gathered[i, 0]
        out[i, 24:48] = gathered[i, 1]
        for k, end in enumerate(ends):
            out[i, 48 + 8 * k : 56 + 8 * k] = end


def residual_kernel(place, tmpl, prev_row, next_row, mixed, *rest):
    raws, out, parts, (rows, total) = rest[:4], rest[4], rest[5:9], rest[9:]
    zh, c, zl, x = place[1], place[2], place[3], place[4]
    low, high = tmpl[zh, :12], tmpl[zh, 12:]
    here = jnp.concatenate([low, high], -1)

    step = jnp.where(c == 0, zh - 1, zh)
    inside = jnp.logical_and(x + step >= 0, x + step < 4)
    chip = jnp.clip(x + step, 0, 3)
    near = jnp.concatenate([mixed[2 * x + 1 - c, 48:56], mixed[2 * x + 1 - c, 56:64]], -1)
    far = jnp.concatenate([mixed[2 * chip + 1 - c, 64:72], mixed[2 * chip + 1 - c, 72:80]], -1)
    far = jnp.where(inside, far, 0.0)
    before, after = jnp.where(c == 0, far, near), jnp.where(c == 0, near, far)
    up = jnp.concatenate([here[1:], after[None]], 0)
    down = jnp.concatenate([before[None], here[:-1]], 0)
    slope_z = (up - down) * 0.5

    line = lax.broadcasted_iota(jnp.int32, (12, 8, WIDE), 1)

    def edge(ref):
        e = jnp.concatenate([ref[zh, :12], ref[zh, 12:]], -1)
        return jnp.broadcast_to(e[:, None, :], (12, 8, WIDE))

    up = jnp.where(line == 7, edge(next_row), pltpu.roll(here, 7, 1))
    down = jnp.where(line == 0, edge(prev_row), pltpu.roll(here, 1, 1))
    slope_y = (up - down) * 0.5
    slope_x = (pltpu.roll(here, WIDE - 1, 2) - pltpu.roll(here, 1, 2)) * 0.5

    slopes = (slope_z, slope_y, slope_x)
    lane = lax.broadcasted_iota(jnp.int32, (12, 8, LANES), 2)
    sum_low = jnp.zeros((12, 8, LANES), F32)
    sum_high = jnp.zeros((12, 8, LANES), F32)
    highs = []
    for s, raw in enumerate(raws):
        warped = here[..., :LANES]
        motion = raw[1] * slopes[0][..., :LANES] + raw[2] * slopes[1][..., :LANES] + raw[3] * slopes[2][..., :LANES]
        r_low = raw[0] - (warped + motion)
        zero_one, two_three = raw[4], raw[5]
        swap_01, swap_23 = pltpu.roll(zero_one, 64, 2), pltpu.roll(two_three, 64, 2)
        motion = swap_01 * slopes[0][..., LANES:] + two_three * slopes[1][..., LANES:] + swap_23 * slopes[2][..., LANES:]
        r_high = zero_one - (here[..., LANES:] + motion)
        rows[12 * s : 12 * s + 12] = r_low
        highs.append(r_high)
        sum_low += r_low
        sum_high += r_high
    for k in range(2):
        rows[48 + 12 * k : 60 + 12 * k] = jnp.where(lane < 64, highs[2 * k], pltpu.roll(highs[2 * k + 1], 64, 2))
    rows[72:84] = sum_low
    rows[84:] = sum_high
    for k in range(12):
        block = jnp.swapaxes(rows[8 * k : 8 * k + 8], 0, 1)
        if k >= 9:
            total[:, 8 * (k - 9) : 8 * (k - 8)] = block
            continue
        for i in range(8):
            x, core = i // 2, i % 2
            for h in range(2):
                out[4 * x + 2 * h + core, 8 * k : 8 * k + 8] = block[i]
    for t, part in enumerate(parts):
        part[...] = total[pl.ds(2 * lax.bitwise_xor(zl // 2, t), 2)]


def slopes_kernel(prev, mine, succ, out, grid):
    for r, ref in enumerate((prev, mine, succ)):
        grid[r, :8] = jnp.zeros((8, WIDE), F32)
        grid[r, 200:] = jnp.zeros((8, WIDE), F32)
        for x in range(4):
            for h in range(2):
                at = 8 + 48 * x + 24 * h
                first, second = (ref[2 * x + c, 24 * h : 24 * h + 24] for c in range(2))
                grid[r, at : at + 24, :LANES] = jnp.concatenate([first[:12], second[:12]], 0)
                grid[r, at : at + 24, LANES:] = jnp.concatenate([first[12:], second[12:]], 0)
    here = grid[1, 8:200]
    low_lane = lax.broadcasted_iota(jnp.int32, (192, LANES), 1) < 64
    slopes = (
        (grid[1, 9:201] - grid[1, 7:199]) * 0.5,
        (grid[2, 8:200] - grid[0, 8:200]) * 0.5,
        (pltpu.roll(here, WIDE - 1, 1) - pltpu.roll(here, 1, 1)) * 0.5,
    )
    for c, a in enumerate(slopes):
        high = a[:, LANES:]
        out[c, :, :LANES] = a[:, :LANES]
        out[c, :, LANES:] = jnp.where(low_lane, high, pltpu.roll(high, 64, 1))


def main_kernel(place, slopes, got, zw, xw, out, force):
    y = place[0]
    for k in range(8):
        at = slice(24 * k, 24 * k + 24)
        for b in range(6):
            r = jnp.concatenate([got[2 * k, 12 * b : 12 * b + 12], got[2 * k + 1, 12 * b : 12 * b + 12]], 0)
            for c in range(3):
                half = slice(0, LANES) if b < 4 else slice(LANES, WIDE)
                force[at, (c * 6 + b) * LANES : (c * 6 + b + 1) * LANES] = r * slopes[c, at, half]

    def times(a1, a0, b1, b0):
        dot = lambda p, q: jnp.dot(p, q, preferred_element_type=F32)
        return dot(a1, b1) + (dot(a1, b0) + dot(a0, b1))

    smooth = times(zw[0], zw[1], *split(force[...]))

    for odd in range(2):
        left = []
        for s in (odd, odd + 2):
            for c in range(3):
                at = c * 6 * LANES
                left.append(
                    jnp.concatenate(
                        [
                            smooth[:, at + s * LANES : at + (s + 1) * LANES],
                            smooth[:, at + (4 + s // 2) * LANES : at + (5 + s // 2) * LANES],
                        ],
                        1,
                    )
                )
        update = times(*split(jnp.concatenate(left, 0)), xw[odd, 0], xw[odd, 1])
        for i, s in enumerate((odd, odd + 2)):
            to = 8 * lax.rem(y + 4 - s, 4)
            for c in range(3):
                for j in range(8):
                    at = (i * 3 + c) * 96 + 12 * j
                    piece = update[at : at + 12]
                    out[to + j, 12 * c : 12 * c + 12, :] = piece[:, :LANES]
                    out[to + j, 36 + 6 * c : 42 + 6 * c, :] = jnp.concatenate(
                        [piece[:6, LANES:], piece[6:, LANES:]], 1
                    )


def unpack_kernel(packed, out):
    for k in range(4):
        rows = slice(8 * k, 8 * k + 8)
        block = jnp.swapaxes(packed[rows], 0, 1)
        for c in range(3):
            out[c, :, rows, :LANES] = block[12 * c : 12 * c + 12]
            high = block[36 + 6 * c : 42 + 6 * c]
            out[c, :6, rows, LANES:] = high[..., :64]
            out[c, 6:, rows, LANES:] = high[..., 64:]


def per_device(image, velocity, template, z_kernel, x_kernel):
    place = jnp.stack([lax.axis_index(a) for a in ("y", "zh", "c", "zl", "x")]).astype(jnp.int32)

    (piece,) = call(piece_kernel, (shape(16, 24, LANES),))(None, template)
    gathered = lax.all_to_all(piece, COL, 0, 0, tiled=True).reshape(8, 2, 24, LANES)

    raws = call(
        pack_kernel, (held(6, 12, 8, LANES), *[shape(6, 12, 8, LANES)] * 3), pin=False
    )(place, image[0], velocity[0])
    raws = list(raws)
    for s in (2, 1, 3):
        raws[s] = lax.ppermute(raws[s], "y", [(i, (i + s) % 4) for i in range(4)])

    prev_row = lax.ppermute(gathered[7], "y", [(i, i + 1) for i in range(3)])
    next_row = lax.ppermute(gathered[0], "y", [(i + 1, i) for i in range(3)])
    tmpl, mixed = call(spread_kernel, (held(2, 24, 8, LANES), shape(8, 80, LANES)))(place, gathered)
    mixed = lax.all_to_all(mixed, ("x", "c"), 0, 0, tiled=True)

    by_row, *parts = call(
        residual_kernel,
        (shape(16, 72, LANES), held(2, 24, LANES), *[shape(2, 24, LANES)] * 3),
        (pltpu.VMEM((96, 8, LANES), F32), pltpu.VMEM((8, 24, LANES), F32)),
    )(place, tmpl, prev_row, next_row, mixed, *raws)
    got = lax.all_to_all(by_row, ("x", "zh", "c"), 0, 0, tiled=True)

    along = [(i, i + 1) for i in range(31)]
    prev = lax.ppermute(mixed, ROW, along)
    succ = lax.ppermute(mixed, ROW, [(j, i) for i, j in along])
    zw, xw = call(
        weights_kernel,
        (pltpu.VMEM((2, 96, 192), BF16), pltpu.VMEM((2, 2, 256, 192), BF16)),
    )(place, z_kernel, x_kernel)

    (slopes,) = call(slopes_kernel, (held(3, 192, WIDE),), (pltpu.VMEM((3, 208, WIDE), F32),))(
        None, prev, mixed, succ
    )
    slopes, *parts[1:] = lax.optimization_barrier((slopes, *parts[1:]))
    (packed,) = call(main_kernel, (shape(32, 54, LANES),), (pltpu.VMEM((192, 18 * LANES), F32),))(
        place, slopes, got, zw, xw
    )

    for t in (1, 2, 3):
        parts[t] = lax.ppermute(parts[t], "zl", [(i, i ^ (2 * t)) for i in range(8)])
    two, odd = sum(parts), lax.axis_index("zl") & 1
    keep = lax.dynamic_index_in_dim(two, odd, 0, False)
    give = lax.dynamic_index_in_dim(two, 1 - odd, 0, False)
    total = keep + lax.ppermute(give, "zl", [(i, i ^ 1) for i in range(8)])
    summed = jnp.concatenate([total[:12], total[12:, :64]], -1)[:, None]
    new_template = template + summed / 32

    back = lax.all_to_all(packed, ROW, 0, 0, tiled=True)
    (out,) = call(unpack_kernel, (shape(3, 12, 32, 192),))(None, back)
    return out[None], new_template


def solution(mesh):
    fine = Mesh(mesh.devices.reshape(4, 8, 4, 2, 2), ("y", "zl", "x", "zh", "c"))
    subj, slab = ("y", "zl"), ("x", "zh", "c")
    in_specs = (
        P(subj, slab, None, None),
        P(subj, None, slab, None, None),
        P(slab, subj, None),
        P(),
        P(),
    )
    out_specs = (P(subj, None, slab, None, None), P(slab, subj, None))
    return jax.shard_map(
        per_device, mesh=fine, in_specs=in_specs, out_specs=out_specs, check_vma=False
    )
```

```python
import jax
import jax.numpy as jnp
from jax import lax
from jax.experimental import pallas as pl
from jax.experimental.pallas import tpu as pltpu
from jax.sharding import Mesh, PartitionSpec as P

ROW = ("y", "x", "c")
COL = ("zl", "zh")
LANES, WIDE = 128, 256
F32 = jnp.float32
BF16 = jnp.bfloat16


def shape(*dims):
    return jax.ShapeDtypeStruct(dims, F32)


def held(*dims):
    return pltpu.VMEM(dims, F32)


def vmem(n):
    return [pl.BlockSpec(memory_space=pltpu.VMEM)] * n


def smem():
    return pl.BlockSpec(memory_space=pltpu.SMEM)


def call(kernel, outs, scratch=(), pin=True):
    def run(place, *args):
        if pin:
            args = [pltpu.with_memory_space_constraint(a, pltpu.VMEM) for a in args]
        first = [] if place is None else [place]
        return pl.pallas_call(
            kernel,
            out_shape=outs,
            in_specs=[*([smem()] * len(first)), *vmem(len(args))],
            out_specs=tuple(vmem(len(outs))),
            scratch_shapes=list(scratch),
        )(*first, *args)

    return run


def piece_kernel(row, out):
    values = row[:, 0, :]
    for i in range(16):
        out[i, :12, :] = values[:, :LANES]
        out[i, 12:, :] = jnp.concatenate([values[:, LANES:], jnp.zeros((12, 64), F32)], 1)


def split(a):
    top = a.astype(BF16)
    return top, (a - top.astype(F32)).astype(BF16)


def weights_kernel(place, zk, xk, zw, xw):
    zrows = [zk[pl.ds(pl.multiple_of(48 * x + 24 * place[1], 8), 24), :] for x in range(4)]
    zw[0], zw[1] = split(jnp.concatenate(zrows, 0))
    xt = xk[...].T
    zeros = jnp.zeros((64, 192), F32)
    for odd in range(2):
        cols = [xt[:LANES], zeros, xt[LANES:]] if odd else [xt[:LANES], xt[LANES:], zeros]
        xw[odd, 0], xw[odd, 1] = split(jnp.concatenate(cols, 0))


def pack_kernel(place, image, velocity, *outs):
    for s, out in enumerate(outs):
        at = pl.multiple_of(8 * lax.rem(place[0] + s, 4), 8)
        rows = pl.ds(at, 8)
        for a in range(4):
            src = image if a == 0 else velocity.at[a - 1]
            out[a] = src[:, rows, :LANES]
        for k in range(2):
            first = image if k == 0 else velocity.at[1]
            second = velocity.at[2 * k]
            out[4 + k] = jnp.concatenate([first[:, rows, LANES:], second[:, rows, LANES:]], -1)


def rows_kernel(gathered, tmpl):
    for h in range(2):
        for k in range(3):
            tmpl[h, 8 * k : 8 * k + 8] = jnp.swapaxes(gathered[:, h, 8 * k : 8 * k + 8], 0, 1)


def spread_kernel(place, gathered, out):
    zh, c = place[1], place[2]

    def plane(h, p):
        return jnp.concatenate([gathered[i, h, p : p + 1] for i in range(8)], 0)

    def end(last, h, high):
        at = 12 * high
        first_half = jnp.where(last == 1, plane(0, at + 11), plane(0, at))
        second_half = jnp.where(last == 1, plane(1, at + 11), plane(1, at))
        return jnp.where(h == 0, first_half, second_half)

    ends = [end(1 - c, zh, 0), end(1 - c, zh, 1), end(c, 1 - zh, 0), end(c, 1 - zh, 1)]
    for i in range(8):
        out[i, :24] = gathered[i, 0]
        out[i, 24:48] = gathered[i, 1]
        for k, e in enumerate(ends):
            out[i, 48 + 8 * k : 56 + 8 * k] = e


def residual_kernel(place, tmpl, prev_row, next_row, mixed, *rest):
    raws, out, parts, (rows, total) = rest[:4], rest[4], rest[5:9], rest[9:]
    zh, c, zl, x = place[1], place[2], place[3], place[4]
    low, high = tmpl[zh, :12], tmpl[zh, 12:]
    here = jnp.concatenate([low, high], -1)

    step = jnp.where(c == 0, zh - 1, zh)
    inside = jnp.logical_and(x + step >= 0, x + step < 4)
    chip = jnp.clip(x + step, 0, 3)
    near = jnp.concatenate([mixed[2 * x + 1 - c, 48:56], mixed[2 * x + 1 - c, 56:64]], -1)
    far = jnp.concatenate([mixed[2 * chip + 1 - c, 64:72], mixed[2 * chip + 1 - c, 72:80]], -1)
    far = jnp.where(inside, far, 0.0)
    before, after = jnp.where(c == 0, far, near), jnp.where(c == 0, near, far)
    up = jnp.concatenate([here[1:], after[None]], 0)
    down = jnp.concatenate([before[None], here[:-1]], 0)
    slope_z = (up - down) * 0.5

    line = lax.broadcasted_iota(jnp.int32, (12, 8, WIDE), 1)

    def edge(ref):
        e = jnp.concatenate([ref[zh, :12], ref[zh, 12:]], -1)
        return jnp.broadcast_to(e[:, None, :], (12, 8, WIDE))

    up = jnp.where(line == 7, edge(next_row), pltpu.roll(here, 7, 1))
    down = jnp.where(line == 0, edge(prev_row), pltpu.roll(here, 1, 1))
    slope_y = (up - down) * 0.5
    slope_x = (pltpu.roll(here, WIDE - 1, 2) - pltpu.roll(here, 1, 2)) * 0.5

    slopes = (slope_z, slope_y, slope_x)
    lane = lax.broadcasted_iota(jnp.int32, (12, 8, LANES), 2)
    sum_low = jnp.zeros((12, 8, LANES), F32)
    sum_high = jnp.zeros((12, 8, LANES), F32)
    highs = []
    for s, raw in enumerate(raws):
        warped = here[..., :LANES]
        motion = raw[1] * slopes[0][..., :LANES] + raw[2] * slopes[1][..., :LANES] + raw[3] * slopes[2][..., :LANES]
        r_low = raw[0] - (warped + motion)
        zero_one, two_three = raw[4], raw[5]
        swap_01, swap_23 = pltpu.roll(zero_one, 64, 2), pltpu.roll(two_three, 64, 2)
        motion = swap_01 * slopes[0][..., LANES:] + two_three * slopes[1][..., LANES:] + swap_23 * slopes[2][..., LANES:]
        r_high = zero_one - (here[..., LANES:] + motion)
        rows[12 * s : 12 * s + 12] = r_low
        highs.append(r_high)
        sum_low += r_low
        sum_high += r_high
    for k in range(2):
        rows[48 + 12 * k : 60 + 12 * k] = jnp.where(lane < 64, highs[2 * k], pltpu.roll(highs[2 * k + 1], 64, 2))
    rows[72:84] = sum_low
    rows[84:] = sum_high
    for k in range(12):
        block = jnp.swapaxes(rows[8 * k : 8 * k + 8], 0, 1)
        if k >= 9:
            total[:, 8 * (k - 9) : 8 * (k - 8)] = block
            continue
        for i in range(8):
            x, core = i // 2, i % 2
            for h in range(2):
                out[4 * x + 2 * h + core, 8 * k : 8 * k + 8] = block[i]
    for t, part in enumerate(parts):
        part[...] = total[pl.ds(2 * lax.bitwise_xor(zl // 2, t), 2)]


def slopes_kernel(prev, mine, succ, out, grid):
    for r, ref in enumerate((prev, mine, succ)):
        grid[r, :8] = jnp.zeros((8, WIDE), F32)
        grid[r, 200:] = jnp.zeros((8, WIDE), F32)
        for x in range(4):
            for h in range(2):
                at = 8 + 48 * x + 24 * h
                first, second = (ref[2 * x + c, 24 * h : 24 * h + 24] for c in range(2))
                grid[r, at : at + 24, :LANES] = jnp.concatenate([first[:12], second[:12]], 0)
                grid[r, at : at + 24, LANES:] = jnp.concatenate([first[12:], second[12:]], 0)
    here = grid[1, 8:200]
    low_lane = lax.broadcasted_iota(jnp.int32, (192, LANES), 1) < 64
    slopes = (
        (grid[1, 9:201] - grid[1, 7:199]) * 0.5,
        (grid[2, 8:200] - grid[0, 8:200]) * 0.5,
        (pltpu.roll(here, WIDE - 1, 1) - pltpu.roll(here, 1, 1)) * 0.5,
    )
    for c, a in enumerate(slopes):
        high = a[:, LANES:]
        out[c, :, :LANES] = a[:, :LANES]
        out[c, :, LANES:] = jnp.where(low_lane, high, pltpu.roll(high, 64, 1))


def main_kernel(place, slopes, got, zw, xw, out, force):
    y = place[0]
    for k in range(8):
        at = slice(24 * k, 24 * k + 24)
        for b in range(6):
            r = jnp.concatenate([got[2 * k, 12 * b : 12 * b + 12], got[2 * k + 1, 12 * b : 12 * b + 12]], 0)
            for c in range(3):
                half = slice(0, LANES) if b < 4 else slice(LANES, WIDE)
                force[at, (c * 6 + b) * LANES : (c * 6 + b + 1) * LANES] = r * slopes[c, at, half]

    def times(a1, a0, b1, b0):
        dot = lambda p, q: jnp.dot(p, q, preferred_element_type=F32)
        return dot(a1, b1) + (dot(a1, b0) + dot(a0, b1))

    smooth = times(zw[0], zw[1], *split(force[...]))

    for odd in range(2):
        left = []
        for s in (odd, odd + 2):
            for c in range(3):
                at = c * 6 * LANES
                left.append(
                    jnp.concatenate(
                        [
                            smooth[:, at + s * LANES : at + (s + 1) * LANES],
                            smooth[:, at + (4 + s // 2) * LANES : at + (5 + s // 2) * LANES],
                        ],
                        1,
                    )
                )
        update = times(*split(jnp.concatenate(left, 0)), xw[odd, 0], xw[odd, 1])
        for i, s in enumerate((odd, odd + 2)):
            to = 8 * lax.rem(y + 4 - s, 4)
            for c in range(3):
                for j in range(8):
                    at = (i * 3 + c) * 96 + 12 * j
                    piece = update[at : at + 12]
                    out[to + j, 12 * c : 12 * c + 12, :] = piece[:, :LANES]
                    out[to + j, 36 + 6 * c : 42 + 6 * c, :] = jnp.concatenate(
                        [piece[:6, LANES:], piece[6:, LANES:]], 1
                    )


def unpack_kernel(packed, out):
    for k in range(4):
        rows = slice(8 * k, 8 * k + 8)
        block = jnp.swapaxes(packed[rows], 0, 1)
        for c in range(3):
            out[c, :, rows, :LANES] = block[12 * c : 12 * c + 12]
            high = block[36 + 6 * c : 42 + 6 * c]
            out[c, :6, rows, LANES:] = high[..., :64]
            out[c, 6:, rows, LANES:] = high[..., 64:]


def per_device(image, velocity, template, z_kernel, x_kernel):
    place = jnp.stack([lax.axis_index(a) for a in ("y", "zh", "c", "zl", "x")]).astype(jnp.int32)

    (piece,) = call(piece_kernel, (shape(16, 24, LANES),))(None, template)
    gathered = lax.all_to_all(piece, COL, 0, 0, tiled=True).reshape(8, 2, 24, LANES)

    raws = call(
        pack_kernel, (held(6, 12, 8, LANES), *[shape(6, 12, 8, LANES)] * 3), pin=False
    )(place, image[0], velocity[0])
    raws = list(raws)
    for s in (2, 1, 3):
        raws[s] = lax.ppermute(raws[s], "y", [(i, (i + s) % 4) for i in range(4)])

    prev_row = lax.ppermute(gathered[7], "y", [(i, i + 1) for i in range(3)])
    next_row = lax.ppermute(gathered[0], "y", [(i + 1, i) for i in range(3)])
    (mixed,) = call(spread_kernel, (shape(8, 80, LANES),))(place, gathered)
    (tmpl,) = call(rows_kernel, (held(2, 24, 8, LANES),))(None, gathered)
    mixed = lax.all_to_all(mixed, ("x", "c"), 0, 0, tiled=True)

    by_row, *parts = call(
        residual_kernel,
        (shape(16, 72, LANES), held(2, 24, LANES), *[shape(2, 24, LANES)] * 3),
        (pltpu.VMEM((96, 8, LANES), F32), pltpu.VMEM((8, 24, LANES), F32)),
    )(place, tmpl, prev_row, next_row, mixed, *raws)
    got = lax.all_to_all(by_row, ("x", "zh", "c"), 0, 0, tiled=True)

    along = [(i, i + 1) for i in range(31)]
    prev = lax.ppermute(mixed, ROW, along)
    succ = lax.ppermute(mixed, ROW, [(j, i) for i, j in along])
    zw, xw = call(
        weights_kernel,
        (pltpu.VMEM((2, 96, 192), BF16), pltpu.VMEM((2, 2, 256, 192), BF16)),
    )(place, z_kernel, x_kernel)

    (slopes,) = call(slopes_kernel, (held(3, 192, WIDE),), (pltpu.VMEM((3, 208, WIDE), F32),))(
        None, prev, mixed, succ
    )
    slopes, *parts[1:] = lax.optimization_barrier((slopes, *parts[1:]))
    (packed,) = call(main_kernel, (shape(32, 54, LANES),), (pltpu.VMEM((192, 18 * LANES), F32),))(
        place, slopes, got, zw, xw
    )

    for t in (1, 2, 3):
        parts[t] = lax.ppermute(parts[t], "zl", [(i, i ^ (2 * t)) for i in range(8)])
    two, odd = sum(parts), lax.axis_index("zl") & 1
    keep = lax.dynamic_index_in_dim(two, odd, 0, False)
    give = lax.dynamic_index_in_dim(two, 1 - odd, 0, False)
    total = keep + lax.ppermute(give, "zl", [(i, i ^ 1) for i in range(8)])
    summed = jnp.concatenate([total[:12], total[12:, :64]], -1)[:, None]
    new_template = template + summed / 32

    back = lax.all_to_all(packed, ROW, 0, 0, tiled=True)
    (out,) = call(unpack_kernel, (shape(3, 12, 32, 192),))(None, back)
    return out[None], new_template


def solution(mesh):
    fine = Mesh(mesh.devices.reshape(4, 8, 4, 2, 2), ("y", "zl", "x", "zh", "c"))
    subj, slab = ("y", "zl"), ("x", "zh", "c")
    in_specs = (
        P(subj, slab, None, None),
        P(subj, None, slab, None, None),
        P(slab, subj, None),
        P(),
        P(),
    )
    out_specs = (P(subj, None, slab, None, None), P(slab, subj, None))
    return jax.shard_map(
        per_device, mesh=fine, in_specs=in_specs, out_specs=out_specs, check_vma=False
    )
```

```python
import jax
import jax.numpy as jnp
from jax import lax
from jax.experimental import pallas as pl
from jax.experimental.pallas import tpu as pltpu
from jax.sharding import Mesh, PartitionSpec as P

ROW = ("y", "x", "c")
COL = ("zl", "zh")
LANES, WIDE = 128, 256
F32 = jnp.float32
BF16 = jnp.bfloat16


def shape(*dims):
    return jax.ShapeDtypeStruct(dims, F32)


def held(*dims):
    return pltpu.VMEM(dims, F32)


def vmem(n):
    return [pl.BlockSpec(memory_space=pltpu.VMEM)] * n


def smem():
    return pl.BlockSpec(memory_space=pltpu.SMEM)


def call(kernel, outs, scratch=(), pin=True):
    def run(place, *args):
        if pin:
            args = [pltpu.with_memory_space_constraint(a, pltpu.VMEM) for a in args]
        first = [] if place is None else [place]
        return pl.pallas_call(
            kernel,
            out_shape=outs,
            in_specs=[*([smem()] * len(first)), *vmem(len(args))],
            out_specs=tuple(vmem(len(outs))),
            scratch_shapes=list(scratch),
        )(*first, *args)

    return run


def piece_kernel(row, out):
    values = row[:, 0, :]
    for i in range(16):
        out[i, :12, :] = values[:, :LANES]
        out[i, 12:, :] = jnp.concatenate([values[:, LANES:], jnp.zeros((12, 64), F32)], 1)


def split(a):
    top = a.astype(BF16)
    return top, (a - top.astype(F32)).astype(BF16)


def weights_kernel(place, zk, xk, zw, xw):
    zrows = [zk[pl.ds(pl.multiple_of(48 * x + 24 * place[1], 8), 24), :] for x in range(4)]
    zw[0], zw[1] = split(jnp.concatenate(zrows, 0))
    xt = xk[...].T
    zeros = jnp.zeros((64, 192), F32)
    for odd in range(2):
        cols = [xt[:LANES], zeros, xt[LANES:]] if odd else [xt[:LANES], xt[LANES:], zeros]
        xw[odd, 0], xw[odd, 1] = split(jnp.concatenate(cols, 0))


def pack_kernel(place, image, velocity, *outs):
    for s, out in enumerate(outs):
        at = pl.multiple_of(8 * lax.rem(place[0] + s, 4), 8)
        rows = pl.ds(at, 8)
        for a in range(4):
            src = image if a == 0 else velocity.at[a - 1]
            out[a] = src[:, rows, :LANES]
        for k in range(2):
            first = image if k == 0 else velocity.at[1]
            second = velocity.at[2 * k]
            out[4 + k] = jnp.concatenate([first[:, rows, LANES:], second[:, rows, LANES:]], -1)


def rows_kernel(gathered, tmpl):
    for h in range(2):
        for k in range(3):
            tmpl[h, 8 * k : 8 * k + 8] = jnp.swapaxes(gathered[:, h, 8 * k : 8 * k + 8], 0, 1)


def spread_kernel(place, gathered, out):
    zh, c = place[1], place[2]

    def plane(h, p):
        return jnp.concatenate([gathered[i, h, p : p + 1] for i in range(8)], 0)

    def end(last, h, high):
        at = 12 * high
        first_half = jnp.where(last == 1, plane(0, at + 11), plane(0, at))
        second_half = jnp.where(last == 1, plane(1, at + 11), plane(1, at))
        return jnp.where(h == 0, first_half, second_half)

    ends = [end(1 - c, zh, 0), end(1 - c, zh, 1), end(c, 1 - zh, 0), end(c, 1 - zh, 1)]
    for i in range(8):
        out[i, :24] = gathered[i, 0]
        out[i, 24:48] = gathered[i, 1]
        for k, e in enumerate(ends):
            out[i, 48 + 8 * k : 56 + 8 * k] = e


def residual_kernel(place, tmpl, prev_row, next_row, mixed, *rest):
    raws, out, parts, (rows, total) = rest[:4], rest[4], rest[5:9], rest[9:]
    zh, c, zl, x = place[1], place[2], place[3], place[4]
    low, high = tmpl[zh, :12], tmpl[zh, 12:]
    here = jnp.concatenate([low, high], -1)

    step = jnp.where(c == 0, zh - 1, zh)
    inside = jnp.logical_and(x + step >= 0, x + step < 4)
    chip = jnp.clip(x + step, 0, 3)
    near = jnp.concatenate([mixed[2 * x + 1 - c, 48:56], mixed[2 * x + 1 - c, 56:64]], -1)
    far = jnp.concatenate([mixed[2 * chip + 1 - c, 64:72], mixed[2 * chip + 1 - c, 72:80]], -1)
    far = jnp.where(inside, far, 0.0)
    before, after = jnp.where(c == 0, far, near), jnp.where(c == 0, near, far)
    up = jnp.concatenate([here[1:], after[None]], 0)
    down = jnp.concatenate([before[None], here[:-1]], 0)
    slope_z = (up - down) * 0.5

    line = lax.broadcasted_iota(jnp.int32, (12, 8, WIDE), 1)

    def edge(ref):
        e = jnp.concatenate([ref[zh, :12], ref[zh, 12:]], -1)
        return jnp.broadcast_to(e[:, None, :], (12, 8, WIDE))

    up = jnp.where(line == 7, edge(next_row), pltpu.roll(here, 7, 1))
    down = jnp.where(line == 0, edge(prev_row), pltpu.roll(here, 1, 1))
    slope_y = (up - down) * 0.5
    slope_x = (pltpu.roll(here, WIDE - 1, 2) - pltpu.roll(here, 1, 2)) * 0.5

    slopes = (slope_z, slope_y, slope_x)
    lane = lax.broadcasted_iota(jnp.int32, (12, 8, LANES), 2)
    sum_low = jnp.zeros((12, 8, LANES), F32)
    sum_high = jnp.zeros((12, 8, LANES), F32)
    highs = []
    for s, raw in enumerate(raws):
        warped = here[..., :LANES]
        motion = raw[1] * slopes[0][..., :LANES] + raw[2] * slopes[1][..., :LANES] + raw[3] * slopes[2][..., :LANES]
        r_low = raw[0] - (warped + motion)
        zero_one, two_three = raw[4], raw[5]
        swap_01, swap_23 = pltpu.roll(zero_one, 64, 2), pltpu.roll(two_three, 64, 2)
        motion = swap_01 * slopes[0][..., LANES:] + two_three * slopes[1][..., LANES:] + swap_23 * slopes[2][..., LANES:]
        r_high = zero_one - (here[..., LANES:] + motion)
        rows[12 * s : 12 * s + 12] = r_low
        highs.append(r_high)
        sum_low += r_low
        sum_high += r_high
    for k in range(2):
        rows[48 + 12 * k : 60 + 12 * k] = jnp.where(lane < 64, highs[2 * k], pltpu.roll(highs[2 * k + 1], 64, 2))
    rows[72:84] = sum_low
    rows[84:] = sum_high
    for k in range(12):
        block = jnp.swapaxes(rows[8 * k : 8 * k + 8], 0, 1)
        if k >= 9:
            total[:, 8 * (k - 9) : 8 * (k - 8)] = block
            continue
        for i in range(8):
            x, core = i // 2, i % 2
            for h in range(2):
                out[4 * x + 2 * h + core, 8 * k : 8 * k + 8] = block[i]
    for t, part in enumerate(parts):
        part[...] = total[pl.ds(2 * lax.bitwise_xor(zl // 2, t), 2)]


def slopes_kernel(prev, mine, succ, out, grid):
    for r, ref in enumerate((prev, mine, succ)):
        grid[r, :8] = jnp.zeros((8, WIDE), F32)
        grid[r, 200:] = jnp.zeros((8, WIDE), F32)
        for x in range(4):
            for h in range(2):
                at = 8 + 48 * x + 24 * h
                first, second = (ref[2 * x + c, 24 * h : 24 * h + 24] for c in range(2))
                grid[r, at : at + 24, :LANES] = jnp.concatenate([first[:12], second[:12]], 0)
                grid[r, at : at + 24, LANES:] = jnp.concatenate([first[12:], second[12:]], 0)
    here = grid[1, 8:200]
    low_lane = lax.broadcasted_iota(jnp.int32, (192, LANES), 1) < 64
    slopes = (
        (grid[1, 9:201] - grid[1, 7:199]) * 0.5,
        (grid[2, 8:200] - grid[0, 8:200]) * 0.5,
        (pltpu.roll(here, WIDE - 1, 1) - pltpu.roll(here, 1, 1)) * 0.5,
    )
    for c, a in enumerate(slopes):
        high = a[:, LANES:]
        out[c, :, :LANES] = a[:, :LANES]
        out[c, :, LANES:] = jnp.where(low_lane, high, pltpu.roll(high, 64, 1))


def main_kernel(place, slopes, got, zw, xw, out, force):
    y = place[0]
    for x in range(4):
        at = slice(48 * x, 48 * x + 48)
        for b in range(6):
            r = jnp.concatenate([got[4 * x + k, 12 * b : 12 * b + 12] for k in range(4)], 0)
            for c in range(3):
                half = slice(0, LANES) if b < 4 else slice(LANES, WIDE)
                to = slice((c * 6 + b) * LANES, (c * 6 + b + 1) * LANES)
                force[0, at, to], force[1, at, to] = split(r * slopes[c, at, half])

    def times(a1, a0, b1, b0):
        dot = lambda p, q: jnp.dot(p, q, preferred_element_type=F32)
        return dot(a1, b1) + (dot(a1, b0) + dot(a0, b1))

    smooth = times(zw[0], zw[1], force[0], force[1])

    for odd in range(2):
        left = []
        for s in (odd, odd + 2):
            for c in range(3):
                at = c * 6 * LANES
                left.append(
                    jnp.concatenate(
                        [
                            smooth[:, at + s * LANES : at + (s + 1) * LANES],
                            smooth[:, at + (4 + s // 2) * LANES : at + (5 + s // 2) * LANES],
                        ],
                        1,
                    )
                )
        update = times(*split(jnp.concatenate(left, 0)), xw[odd, 0], xw[odd, 1])
        for i, s in enumerate((odd, odd + 2)):
            to = 8 * lax.rem(y + 4 - s, 4)
            for c in range(3):
                for j in range(8):
                    at = (i * 3 + c) * 96 + 12 * j
                    piece = update[at : at + 12]
                    out[to + j, 12 * c : 12 * c + 12, :] = piece[:, :LANES]
                    out[to + j, 36 + 6 * c : 42 + 6 * c, :] = jnp.concatenate(
                        [piece[:6, LANES:], piece[6:, LANES:]], 1
                    )


def unpack_kernel(packed, out):
    for k in range(4):
        rows = slice(8 * k, 8 * k + 8)
        block = jnp.swapaxes(packed[rows], 0, 1)
        for c in range(3):
            out[c, :, rows, :LANES] = block[12 * c : 12 * c + 12]
            high = block[36 + 6 * c : 42 + 6 * c]
            out[c, :6, rows, LANES:] = high[..., :64]
            out[c, 6:, rows, LANES:] = high[..., 64:]


def per_device(image, velocity, template, z_kernel, x_kernel):
    place = jnp.stack([lax.axis_index(a) for a in ("y", "zh", "c", "zl", "x")]).astype(jnp.int32)

    (piece,) = call(piece_kernel, (shape(16, 24, LANES),))(None, template)
    gathered = lax.all_to_all(piece, COL, 0, 0, tiled=True).reshape(8, 2, 24, LANES)

    raws = call(
        pack_kernel, (held(6, 12, 8, LANES), *[shape(6, 12, 8, LANES)] * 3), pin=False
    )(place, image[0], velocity[0])
    raws = list(raws)
    for s in (2, 1, 3):
        raws[s] = lax.ppermute(raws[s], "y", [(i, (i + s) % 4) for i in range(4)])

    prev_row = lax.ppermute(gathered[7], "y", [(i, i + 1) for i in range(3)])
    next_row = lax.ppermute(gathered[0], "y", [(i + 1, i) for i in range(3)])
    (mixed,) = call(spread_kernel, (shape(8, 80, LANES),))(place, gathered)
    (tmpl,) = call(rows_kernel, (held(2, 24, 8, LANES),))(None, gathered)
    mixed = lax.all_to_all(mixed, ("x", "c"), 0, 0, tiled=True)

    by_row, *parts = call(
        residual_kernel,
        (shape(16, 72, LANES), held(2, 24, LANES), *[shape(2, 24, LANES)] * 3),
        (pltpu.VMEM((96, 8, LANES), F32), pltpu.VMEM((8, 24, LANES), F32)),
    )(place, tmpl, prev_row, next_row, mixed, *raws)
    got = lax.all_to_all(by_row, ("x", "zh", "c"), 0, 0, tiled=True)

    along = [(i, i + 1) for i in range(31)]
    prev = lax.ppermute(mixed, ROW, along)
    succ = lax.ppermute(mixed, ROW, [(j, i) for i, j in along])
    zw, xw = call(
        weights_kernel,
        (pltpu.VMEM((2, 96, 192), BF16), pltpu.VMEM((2, 2, 256, 192), BF16)),
    )(place, z_kernel, x_kernel)

    (slopes,) = call(slopes_kernel, (held(3, 192, WIDE),), (pltpu.VMEM((3, 208, WIDE), F32),))(
        None, prev, mixed, succ
    )
    slopes, *parts[1:] = lax.optimization_barrier((slopes, *parts[1:]))
    (packed,) = call(main_kernel, (shape(32, 54, LANES),), (pltpu.VMEM((2, 192, 18 * LANES), BF16),))(
        place, slopes, got, zw, xw
    )

    for t in (1, 2, 3):
        parts[t] = lax.ppermute(parts[t], "zl", [(i, i ^ (2 * t)) for i in range(8)])
    two, odd = sum(parts), lax.axis_index("zl") & 1
    keep = lax.dynamic_index_in_dim(two, odd, 0, False)
    give = lax.dynamic_index_in_dim(two, 1 - odd, 0, False)
    total = keep + lax.ppermute(give, "zl", [(i, i ^ 1) for i in range(8)])
    summed = jnp.concatenate([total[:12], total[12:, :64]], -1)[:, None]
    new_template = template + summed / 32

    back = lax.all_to_all(packed, ROW, 0, 0, tiled=True)
    (out,) = call(unpack_kernel, (shape(3, 12, 32, 192),))(None, back)
    return out[None], new_template


def solution(mesh):
    fine = Mesh(mesh.devices.reshape(4, 8, 4, 2, 2), ("y", "zl", "x", "zh", "c"))
    subj, slab = ("y", "zl"), ("x", "zh", "c")
    in_specs = (
        P(subj, slab, None, None),
        P(subj, None, slab, None, None),
        P(slab, subj, None),
        P(),
        P(),
    )
    out_specs = (P(subj, None, slab, None, None), P(slab, subj, None))
    return jax.shard_map(
        per_device, mesh=fine, in_specs=in_specs, out_specs=out_specs, check_vma=False
    )
```
